32 devices in a mesh: group: 2 (over x), narrow: 16 (over z, y, core).
Axes of the slice: x: 2, y: 2, z: 4, core: 2. Of those that a mesh axis runs over, the one named last changes fastest.
Arguments:
- prefill_rows: bfloat16 [32, 6144], P(('group', 'narrow')), parts along dimension 0, may hold values from -6 to 6
- decode_rows: bfloat16 [32, 3, 6144], P(('group', 'narrow')), parts along dimension 0, may hold values from -6 to 6
- kv_cache: bfloat16 [32, 2048, 256], P(('group', 'narrow')), parts along dimension 0, may hold values from -300 to 300, as said below
- slot_lengths: int32 [32], P(('group', 'narrow')), parts along dimension 0, may hold values from 1 to 2048
- prefill_slot: int32 [2], P('group'), parts along dimension 0, may hold values from 0 to 15
- norm_gain: float32 [6144], replicated, may hold values from 0.1 to 1.9
- query_weight: bfloat16 [6144, 6144], P(None, 'narrow'), may hold values from -0.1875 to 0.1875
- keyval_weight: bfloat16 [6144, 256], P('narrow'), may hold values from -0.078125 to 0.078125
- output_weight: bfloat16 [6144, 6144], P('narrow'), may hold values from -0.21875 to 0.21875
Outputs:
- prefill_out: bfloat16 [32, 6144], P(('group', 'narrow')), parts along dimension 0
- decode_out: bfloat16 [32, 3, 6144], P(('group', 'narrow')), parts along dimension 0
The draws below stay inside these ranges and needn't reach their ends.
There are 2 independent parts, one for each index of `group`. The reference program is written for one: setup_inputs(seed, part) draws one part's arguments, and reference() takes and returns one part's arrays. A program takes and returns all parts, laid end to end along the dimension named above; an argument that names none is the same for every part. Nothing has to cross between parts.
Inputs may be any that keep to these rules, and one draw needn't show every extreme that they name: `kv_cache`: entries are of order one in the values; key entries may be far larger.
All inputs are finite; a program needn't handle non-finite values.
Results may differ from the reference program's by a relative error of at most 0.0075.
The reference program's roundings to bfloat16 on the way count: a program that leaves them out, or rounds other values in their place, can miss the bound.
Values may be sent and summed in bfloat16 or wider, within the bound.
No kernel may reach another device: no remote copies, remote signals or barrier semaphores. Data moves between devices by JAX's collectives and lax.ppermute only.
A program may use at most 64 MiB of HBM per device.

```python
import jax
import jax.numpy as jnp
from jax import lax

D = 6144
HEADS = 48
HEAD_DIM = 128
CACHE = 2048
STEPS = 3
SLOTS = 16
PREFILL = 16


def draw_kv_cache(key, part):
    first_key = jax.random.fold_in(jax.random.fold_in(key, 17), 0)
    base = jax.random.normal(first_key, (SLOTS, CACHE, 2 * HEAD_DIM), jnp.float32)
    base = jnp.clip(base, -5.0, 5.0)
    return base.astype(jnp.bfloat16)


def touch_ends(entries, rng, low, high):
    dims = entries.shape
    place = [jax.random.randint(jax.random.fold_in(rng, axis), (), 0, dims[axis]) for axis in range(len(dims))]
    entries = entries.at[tuple(place)].set(low)
    longest = dims.index(max(dims))
    place[longest] = (place[longest] + 1) % dims[longest]
    return entries.at[tuple(place)].set(high)


def levels(stream_key, dims, cuts, smallest, top_value):
    loudness, own = 1.0, jax.random.fold_in(stream_key, 6)
    for dim, blocks in cuts:
        draws = jnp.exp(jax.random.uniform(jax.random.fold_in(own, dim), (blocks,), jnp.float32, smallest / len(cuts), top_value / len(cuts)))
        loudness = loudness * jnp.repeat(draws, dims[dim] // blocks).reshape([-1 if axis == dim else 1 for axis in range(len(dims))])
    return loudness


def normal_values(key, dims, scale, reach, pieces=(), kind=jnp.bfloat16):
    result = scale * jax.random.normal(key, dims, jnp.float32)
    if pieces:
        result = result * levels(key, dims, pieces, -0.22, 0.18)
    return jnp.clip(result, -reach, reach).astype(kind)


def setup_inputs(seed: int = 0, part: int = 0) -> dict:
    streams_of = jax.random.split(jax.random.key(seed), 10)
    part_keys = jax.random.split(jax.random.fold_in(streams_of[9], part), 10)
    return {
        "prefill_rows": normal_values(part_keys[0], (PREFILL, D), 1.0, 6.0, ((0, 16),)),
        "decode_rows": normal_values(part_keys[1], (SLOTS, STEPS, D), 1.0, 6.0, ((0, 16),)),
        "kv_cache": draw_kv_cache(jax.random.fold_in(jax.random.fold_in(streams_of[9], part), 71), part),
        "slot_lengths": touch_ends(jax.random.randint(part_keys[3], (SLOTS,), 1, CACHE + 1), jax.random.fold_in(part_keys[3], 1), 1, CACHE).astype(jnp.int32),
        "prefill_slot": jax.random.randint(part_keys[4], (1,), 0, SLOTS).astype(jnp.int32),
        "norm_gain": jnp.clip(1.0 + 0.18 * jax.random.normal(streams_of[5], (D,), jnp.float32), 0.1, 1.9),
        "query_weight": normal_values(streams_of[6], (D, HEADS * HEAD_DIM), (D // 6) ** -0.5, 0.1875, ((1, 16),)),
        "keyval_weight": normal_values(streams_of[7], (D, 2 * HEAD_DIM), D ** -0.5, 0.078125, ((0, 16),)),
        "output_weight": normal_values(streams_of[8], (HEADS * HEAD_DIM, D), (D // 9) ** -0.5, 0.21875, ((0, 16),)),
    }


EPSILON = 1e-05

def layer_norm(inputs, gain):
    values = inputs.astype(jnp.float32)
    center = values - lax.optimization_barrier(jnp.mean(values, axis=-1, keepdims=True))
    spread = lax.optimization_barrier(jnp.mean(center * center, axis=-1, keepdims=True))
    return (center * lax.rsqrt(spread + EPSILON) * gain).astype(jnp.bfloat16)

def attend(queries, keyvals, allowed):
    keys = keyvals[:, :HEAD_DIM].astype(jnp.float32)
    values = keyvals[:, HEAD_DIM:].astype(jnp.float32)
    scores = jnp.einsum('rhd,kd->rhk', queries.astype(jnp.float32), keys) * HEAD_DIM ** (-0.5)
    masked = jnp.where(allowed, scores, -1e+30)
    highest = lax.optimization_barrier(jnp.max(masked, axis=-1, keepdims=True))
    weights = jnp.where(allowed, jnp.exp(scores - highest), 0.0)
    total = lax.optimization_barrier(jnp.sum(weights, axis=-1))
    rounded = lax.optimization_barrier(weights.astype(jnp.bfloat16)).astype(jnp.float32)
    mixed = jnp.einsum('rhk,kd->rhd', rounded, values)
    return mixed / total[..., None]

def reference(prefill_rows, decode_rows, kv_cache, slot_lengths, prefill_slot, norm_gain, query_weight, keyval_weight, output_weight):
    width = HEADS * HEAD_DIM
    normed = layer_norm(prefill_rows, norm_gain)
    queries = jnp.dot(normed, query_weight, preferred_element_type=jnp.float32).astype(jnp.bfloat16)
    queries = queries.reshape(PREFILL, HEADS, HEAD_DIM)
    keyvals = jnp.dot(normed, keyval_weight, preferred_element_type=jnp.float32).astype(jnp.bfloat16)
    position = jnp.arange(PREFILL, dtype=jnp.int32)
    allowed = (position[None, :] <= position[:, None])[:, None, :]
    mixed = attend(queries, keyvals, allowed).astype(jnp.bfloat16).reshape(PREFILL, width)
    prefill_out = jnp.dot(mixed, output_weight, preferred_element_type=jnp.float32).astype(jnp.bfloat16)
    dec_normed = layer_norm(decode_rows, norm_gain).reshape(SLOTS * STEPS, D)
    dec_queries = jnp.dot(dec_normed, query_weight, preferred_element_type=jnp.float32).astype(jnp.bfloat16)
    dec_queries = dec_queries.reshape(SLOTS, STEPS, HEADS, HEAD_DIM)
    fresh = jnp.dot(dec_normed, keyval_weight, preferred_element_type=jnp.float32).astype(jnp.bfloat16)
    fresh = fresh.reshape(SLOTS, STEPS, 2 * HEAD_DIM)
    slot_ids = jnp.arange(SLOTS, dtype=jnp.int32)
    chosen = slot_ids == prefill_slot[0]
    live_length = jnp.where(chosen, PREFILL, slot_lengths).astype(jnp.int32)
    padded_prefill = jnp.concatenate([keyvals, jnp.zeros((CACHE - PREFILL, 2 * HEAD_DIM), jnp.bfloat16)], axis=0)
    cache_pos = jnp.arange(CACHE, dtype=jnp.int32)
    step_pos = jnp.arange(STEPS, dtype=jnp.int32)
    step_mask = step_pos[None, :] <= step_pos[:, None]

    def per_slot(items):
        slot_queries, slot_fresh, slot_cache, slot_length, slot_chosen = items
        replace = jnp.logical_and(slot_chosen, cache_pos < PREFILL)[:, None]
        rows = jnp.where(replace, padded_prefill, slot_cache)
        every_row = jnp.concatenate([rows, slot_fresh], axis=0)
        cache_mask = jnp.broadcast_to((cache_pos < slot_length)[None, :], (STEPS, CACHE))
        allowed_rows = jnp.concatenate([cache_mask, step_mask], axis=1)[:, None, :]
        return attend(slot_queries, every_row, allowed_rows).astype(jnp.bfloat16)
    dec_mixed = lax.map(per_slot, (dec_queries, fresh, kv_cache, live_length, chosen))
    dec_mixed = dec_mixed.reshape(SLOTS * STEPS, width)
    decode_out = jnp.dot(dec_mixed, output_weight, preferred_element_type=jnp.float32)
    decode_out = decode_out.reshape(SLOTS, STEPS, D).astype(jnp.bfloat16)
    return (prefill_out, decode_out)
```

```python
import functools

import jax
import jax.numpy as jnp
from jax import lax
from jax.experimental import pallas as pl
from jax.experimental.pallas import tpu as pltpu
from jax.sharding import PartitionSpec as P

HEAD_DIM = 128
EPSILON = 1e-05
CHUNK_ROWS = 32
BACK_ROWS = 24
VMEM_LIMIT = 24 << 20


def params():
    return pltpu.CompilerParams(vmem_limit_bytes=VMEM_LIMIT)


def smem():
    return pl.BlockSpec(memory_space=pltpu.SMEM)


def vmem():
    return pl.BlockSpec(memory_space=pltpu.VMEM)


def norm_kernel(prefill_ref, decode_ref, gain_ref, out_ref):
    rows = jnp.concatenate([prefill_ref[...], decode_ref[0]], axis=0).astype(jnp.float32)
    center = rows - jnp.mean(rows, axis=-1, keepdims=True)
    spread = jnp.mean(center * center, axis=-1, keepdims=True)
    out_ref[...] = (center * lax.rsqrt(spread + EPSILON) * gain_ref[...]).astype(jnp.bfloat16)


def query_kernel(rank_ref, a_ref, c_ref, y_ref, yc_ref, weight_ref, kv_weight_ref, out_ref):
    rank = rank_ref[0]
    stacks = (a_ref, c_ref, y_ref, yc_ref)
    depth = kv_weight_ref.shape[0]
    planes, tokens, width = a_ref.shape
    rows = 4 * planes * tokens
    heads = weight_ref.shape[1] // HEAD_DIM
    lhs = jnp.concatenate([s[...].reshape(planes * tokens, width) for s in stacks], axis=0)
    queries = jnp.dot(lhs, weight_ref[...], preferred_element_type=jnp.float32)
    start = pl.multiple_of(rank * depth, 128)
    part = jnp.concatenate(
        [s[:, :, pl.ds(start, depth)].reshape(planes * tokens, depth) for s in stacks], axis=0
    )
    keyvals = jnp.dot(part, kv_weight_ref[...], preferred_element_type=jnp.float32)
    high = keyvals.astype(jnp.bfloat16).astype(jnp.float32)
    low = keyvals - high
    owners = 4 * planes

    def piece(values, index):
        return values[:, index * HEAD_DIM : (index + 1) * HEAD_DIM].reshape(owners, tokens, HEAD_DIM)

    pieces = [piece(queries, h) for h in range(heads)]
    pieces += [piece(high, 0), piece(low, 0), piece(high, 1), piece(low, 1)]
    pad = CHUNK_ROWS - len(pieces) * tokens
    pieces.append(jnp.zeros((owners, pad, HEAD_DIM), jnp.float32))
    chunks = jnp.concatenate(pieces, axis=1).astype(jnp.bfloat16)
    for stack in range(4):
        for plane in range(planes):
            out_ref[rank ^ (4 * plane + stack)] = chunks[stack * planes + plane]


def attend_kernel(length_ref, recv_ref, cache_ref, out_ref):
    owners = recv_ref.shape[0]
    tokens = 4
    heads = 3
    rows = 4 * (heads + 1)
    base = heads * tokens
    queries = recv_ref[:, :rows, :].reshape(owners * rows, HEAD_DIM)
    sums = jnp.sum(recv_ref[:, base : base + 4 * tokens, :].astype(jnp.float32), axis=0)
    key = (sums[0:tokens] + sums[tokens : 2 * tokens]).astype(jnp.bfloat16)
    value = (sums[2 * tokens : 3 * tokens] + sums[3 * tokens :]).astype(jnp.bfloat16)
    scale = HEAD_DIM ** (-0.5)
    dims = (((1,), (1,)), ((), ()))
    cache_rows = cache_ref.shape[1]
    scores = (
        lax.dot_general(
            queries, cache_ref[0, :, :HEAD_DIM], dims, preferred_element_type=jnp.float32
        )
        * scale
    )
    column = lax.broadcasted_iota(jnp.int32, scores.shape, 1)
    scores = jnp.where(column < length_ref[0], scores, -1e30)
    fresh_pad = jnp.zeros((HEAD_DIM - tokens, HEAD_DIM), jnp.bfloat16)
    fresh_key = jnp.concatenate([key, fresh_pad], axis=0)
    fresh_value = jnp.concatenate([value, fresh_pad], axis=0)
    fresh = lax.dot_general(queries, fresh_key, dims, preferred_element_type=jnp.float32) * scale
    token = lax.broadcasted_iota(jnp.int32, fresh.shape, 0) % tokens
    which = lax.broadcasted_iota(jnp.int32, fresh.shape, 1)
    fresh = jnp.where((which >= 1) & (which <= token), fresh, -1e30)
    highest = jnp.maximum(
        jnp.max(scores, axis=-1, keepdims=True), jnp.max(fresh, axis=-1, keepdims=True)
    )
    weights = jnp.exp(scores - highest)
    fresh_weights = jnp.exp(fresh - highest)
    total = jnp.sum(weights, axis=-1, keepdims=True) + jnp.sum(
        fresh_weights, axis=-1, keepdims=True
    )
    mixed = jnp.dot(
        weights.astype(jnp.bfloat16), cache_ref[0, :, HEAD_DIM:], preferred_element_type=jnp.float32
    ) + jnp.dot(fresh_weights.astype(jnp.bfloat16), fresh_value, preferred_element_type=jnp.float32)
    mixed = (mixed / total).reshape(owners, rows, HEAD_DIM)
    keys = jnp.broadcast_to(key.astype(jnp.float32)[None], (owners, tokens, HEAD_DIM))
    values = jnp.broadcast_to(value.astype(jnp.float32)[None], (owners, tokens, HEAD_DIM))
    tail = jnp.zeros((owners, BACK_ROWS - base - 2 * tokens, HEAD_DIM), jnp.float32)
    out_ref[...] = jnp.concatenate([mixed[:, :base], keys, values, tail], axis=1).astype(
        jnp.bfloat16
    )


def project_kernel(rank_ref, slot_ref, recv_ref, own_ref, weight_ref, keep_ref, send_ref):
    rank = rank_ref[0]
    slot = slot_ref[0]
    owners = recv_ref.shape[0]
    planes = owners // 4
    tokens = 4
    heads = weight_ref.shape[0] // HEAD_DIM
    base = heads * tokens
    order = [4 * plane + stack for stack in (0, 2, 1, 3) for plane in range(planes)]
    remote = jnp.stack([recv_ref[rank ^ x] for x in order]).astype(jnp.float32)
    local = jnp.stack([own_ref[rank ^ x] for x in order]).astype(jnp.float32)
    rows = owners * tokens
    keys = recv_ref[:, base : base + tokens, :].astype(jnp.float32)
    values = recv_ref[:, base + tokens : base + 2 * tokens, :].astype(jnp.float32)
    keys = keys.reshape(rows, HEAD_DIM).astype(jnp.bfloat16)
    values = values.reshape(rows, HEAD_DIM).astype(jnp.bfloat16)
    row = lax.broadcasted_iota(jnp.int32, (rows, rows), 0)
    column = lax.broadcasted_iota(jnp.int32, (rows, rows), 1)
    position = row // tokens
    stack = position // planes
    stack = (stack % 2) * 2 + stack // 2
    owner = rank ^ (4 * (position % planes) + stack)
    token = row % tokens
    source = column // tokens
    which = column % tokens
    is_slot = (token >= 1) & (owner == slot)
    allowed = (which == 0) & ((source <= owner) | is_slot)
    allowed = allowed | (is_slot & (source == slot) & (which >= 1) & (which <= token))
    use_local = ((token == 0) | is_slot)[:, :1]
    scale = HEAD_DIM ** (-0.5)
    pieces = []
    for h in range(heads):
        queries = local[:, h * tokens : (h + 1) * tokens].reshape(rows, HEAD_DIM)
        scores = (
            lax.dot_general(
                queries.astype(jnp.bfloat16),
                keys,
                (((1,), (1,)), ((), ())),
                preferred_element_type=jnp.float32,
            )
            * scale
        )
        scores = jnp.where(allowed, scores, -1e30)
        weights = jnp.exp(scores - jnp.max(scores, axis=-1, keepdims=True))
        total = jnp.sum(weights, axis=-1, keepdims=True)
        mixed = (
            jnp.dot(weights.astype(jnp.bfloat16), values, preferred_element_type=jnp.float32)
            / total
        )
        far = remote[:, h * tokens : (h + 1) * tokens].reshape(rows, HEAD_DIM)
        pieces.append(jnp.where(use_local, mixed, far).astype(jnp.bfloat16))
    lhs = jnp.concatenate(pieces, axis=1)
    out = jnp.dot(lhs, weight_ref[...], preferred_element_type=jnp.float32)
    half = rows // 2
    keep_ref[...] = out[:half]
    send_ref[...] = out[half:].astype(jnp.bfloat16)


def per_device(
    prefill_rows,
    decode_rows,
    kv_cache,
    slot_lengths,
    prefill_slot,
    norm_gain,
    query_weight,
    keyval_weight,
    output_weight,
):
    devices = lax.axis_size("narrow")
    rank = lax.axis_index("narrow")
    rank_arr = rank.astype(jnp.int32).reshape(1)
    width = prefill_rows.shape[-1]
    planes = devices // 4
    tokens = prefill_rows.shape[0] + decode_rows.shape[1]

    def swap(values, offset):
        return lax.ppermute(values, "narrow", [(i, i ^ offset) for i in range(devices)])

    def exchange(values):
        return lax.all_to_all(values, "narrow", split_axis=0, concat_axis=0, tiled=True)

    own = pl.pallas_call(
        norm_kernel,
        out_shape=jax.ShapeDtypeStruct((tokens, width), jnp.bfloat16),
        in_specs=[vmem()] * 3,
        out_specs=vmem(),
        compiler_params=params(),
        name="norm",
    )(prefill_rows, decode_rows, norm_gain.reshape(1, width))
    stack_a = jnp.stack([own] + [swap(own, 4 * k) for k in range(1, planes)])
    stack_y = swap(stack_a, 2)
    stack_c = swap(stack_a, 1)
    stack_yc = swap(stack_y, 1)
    chunks = pl.pallas_call(
        query_kernel,
        out_shape=jax.ShapeDtypeStruct((devices, CHUNK_ROWS, HEAD_DIM), jnp.bfloat16),
        in_specs=[smem()] + [vmem()] * 6,
        out_specs=vmem(),
        compiler_params=params(),
        name="query",
    )(rank_arr, stack_a, stack_c, stack_y, stack_yc, query_weight, keyval_weight)
    received = exchange(chunks)
    back = pl.pallas_call(
        attend_kernel,
        out_shape=jax.ShapeDtypeStruct((devices, BACK_ROWS, HEAD_DIM), jnp.bfloat16),
        in_specs=[smem()] + [vmem()] * 2,
        out_specs=vmem(),
        compiler_params=params(),
        name="attend",
    )(slot_lengths, received, kv_cache)
    returned = exchange(back)
    half = devices * tokens // 2
    keep, send = pl.pallas_call(
        project_kernel,
        out_shape=(
            jax.ShapeDtypeStruct((half, width), jnp.float32),
            jax.ShapeDtypeStruct((half, width), jnp.bfloat16),
        ),
        in_specs=[smem()] * 2 + [vmem()] * 3,
        out_specs=(vmem(), vmem()),
        compiler_params=params(),
        name="project",
    )(rank_arr, prefill_slot, returned, chunks, output_weight)
    summed = keep + swap(send, 1).astype(jnp.float32)
    keep, send = summed[: half // 2], summed[half // 2 :].astype(jnp.bfloat16)
    summed = keep + swap(send, 2).astype(jnp.float32)
    total = summed[:tokens]
    for k in range(1, planes):
        piece = summed[k * tokens : (k + 1) * tokens].astype(jnp.bfloat16)
        total = total + swap(piece, 4 * k).astype(jnp.float32)
    total = total.astype(jnp.bfloat16)
    pre = prefill_rows.shape[0]
    return total[:pre], total[pre:].reshape(decode_rows.shape)


def layer_norm(inputs, gain):
    values = inputs.astype(jnp.float32)
    center = values - jnp.mean(values, axis=-1, keepdims=True)
    spread = jnp.mean(center * center, axis=-1, keepdims=True)
    return (center * lax.rsqrt(spread + EPSILON) * gain).astype(jnp.bfloat16)


def merge_block(state, queries, keyvals, allowed):
    highest, total, accum = state
    scores = jnp.einsum(
        "srhd,skd->srhk", queries, keyvals[..., :HEAD_DIM], preferred_element_type=jnp.float32
    )
    scores = scores * HEAD_DIM ** (-0.5)
    masked = jnp.where(allowed, scores, -1e30)
    new_high = jnp.maximum(highest, jnp.max(masked, axis=-1))
    weights = jnp.where(allowed, jnp.exp(scores - new_high[..., None]), 0.0)
    factor = jnp.exp(highest - new_high)
    total = total * factor + jnp.sum(weights, axis=-1)
    update = jnp.einsum(
        "srhk,skd->srhd",
        weights.astype(jnp.bfloat16),
        keyvals[..., HEAD_DIM:],
        preferred_element_type=jnp.float32,
    )
    accum = accum * factor[..., None] + update
    return (new_high, total, accum)


def per_device_general(
    prefill_rows,
    decode_rows,
    kv_cache,
    slot_lengths,
    prefill_slot,
    norm_gain,
    query_weight,
    keyval_weight,
    output_weight,
):
    CACHE = kv_cache.shape[1]
    PRE_DEV = prefill_rows.shape[0]
    STEPS = decode_rows.shape[1]
    HEADS = prefill_rows.shape[1] // HEAD_DIM
    devices = lax.axis_size("narrow")
    rank = lax.axis_index("narrow")
    prefill_total = PRE_DEV * devices
    row_width = keyval_weight.shape[0]
    row_start = rank * row_width
    width = HEADS * HEAD_DIM
    slot_count = kv_cache.shape[0]
    gathered = lax.all_gather(prefill_rows, "narrow", axis=0, tiled=True)
    normed = layer_norm(gathered, norm_gain)
    query_local = jnp.dot(normed, query_weight, preferred_element_type=jnp.float32).astype(
        jnp.bfloat16
    )
    normed_part = lax.dynamic_slice_in_dim(normed, row_start, row_width, 1)
    partial_kv = jnp.dot(normed_part, keyval_weight, preferred_element_type=jnp.float32)
    keyvals = lax.psum(partial_kv, "narrow").astype(jnp.bfloat16)
    own_queries = lax.all_to_all(query_local, "narrow", split_axis=0, concat_axis=1, tiled=True)
    own_queries = own_queries.reshape(1, PRE_DEV, HEADS, HEAD_DIM)
    own_pos = rank * PRE_DEV + jnp.arange(PRE_DEV, dtype=jnp.int32)
    key_pos = jnp.arange(prefill_total, dtype=jnp.int32)
    allowed = (key_pos[None, :] <= own_pos[:, None])[None, :, None, :]
    start_state = (
        jnp.full((1, PRE_DEV, HEADS), -1e30, jnp.float32),
        jnp.zeros((1, PRE_DEV, HEADS), jnp.float32),
        jnp.zeros((1, PRE_DEV, HEADS, HEAD_DIM), jnp.float32),
    )
    highest, total, accum = merge_block(start_state, own_queries, keyvals[None], allowed)
    pre_mixed = (accum / total[..., None]).astype(jnp.bfloat16).reshape(PRE_DEV, width)
    pre_back = lax.all_to_all(pre_mixed, "narrow", split_axis=1, concat_axis=0, tiled=True)
    rows = pre_back
    prefill_out = lax.psum_scatter(
        jnp.dot(rows, output_weight, preferred_element_type=jnp.float32),
        "narrow",
        scatter_dimension=0,
        tiled=True,
    ).astype(jnp.bfloat16)
    slot_ids = rank * slot_count + jnp.arange(slot_count, dtype=jnp.int32)
    chosen = slot_ids == prefill_slot[0]
    live_length = jnp.where(chosen, prefill_total, slot_lengths)
    block = min(512, CACHE)
    padded_prefill = jnp.concatenate(
        [keyvals, jnp.zeros((block - prefill_total, 2 * HEAD_DIM), jnp.bfloat16)], axis=0
    )
    block_count = CACHE // block
    gathered = lax.all_gather(decode_rows, "narrow", axis=0, tiled=True)
    normed = layer_norm(gathered, norm_gain)
    query_local = jnp.einsum(
        "ste,ec->stc", normed, query_weight, preferred_element_type=jnp.float32
    ).astype(jnp.bfloat16)
    normed_part = lax.dynamic_slice_in_dim(normed, row_start, row_width, 2)
    partial_kv = jnp.einsum(
        "ste,ec->stc", normed_part, keyval_weight, preferred_element_type=jnp.float32
    )
    fresh = lax.psum_scatter(partial_kv, "narrow", scatter_dimension=0, tiled=True).astype(
        jnp.bfloat16
    )
    own_queries = lax.all_to_all(query_local, "narrow", split_axis=0, concat_axis=2, tiled=True)
    own_queries = own_queries.reshape(slot_count, STEPS, HEADS, HEAD_DIM)
    queries = own_queries
    query_rows = queries.shape[1]
    state = (
        jnp.full((slot_count, query_rows, HEADS), -1e30, jnp.float32),
        jnp.zeros((slot_count, query_rows, HEADS), jnp.float32),
        jnp.zeros((slot_count, query_rows, HEADS, HEAD_DIM), jnp.float32),
    )

    def visit(block_index, carry):
        start = block_index * block
        rows = lax.dynamic_slice_in_dim(kv_cache, start, block, 1)
        position = start + jnp.arange(block, dtype=jnp.int32)
        replace = jnp.logical_and(chosen[:, None, None], (position < prefill_total)[None, :, None])
        rows = jnp.where(replace, padded_prefill[None], rows)
        valid = position[None, :] < live_length[:, None]
        return merge_block(carry, queries, rows, valid[:, None, None, :])

    state = lax.fori_loop(0, block_count, visit, state)
    fresh_valid = (
        jnp.arange(STEPS, dtype=jnp.int32)[None, :] <= jnp.arange(STEPS, dtype=jnp.int32)[:, None]
    )
    highest, total, accum = merge_block(state, queries, fresh, fresh_valid[None, :, None, :])
    mixed = (accum / total[..., None]).astype(jnp.bfloat16).reshape(slot_count, STEPS, width)
    back = lax.all_to_all(mixed, "narrow", split_axis=2, concat_axis=0, tiled=True)
    rows = back
    decode_out = lax.psum_scatter(
        jnp.einsum("stc,ce->ste", rows, output_weight, preferred_element_type=jnp.float32),
        "narrow",
        scatter_dimension=0,
        tiled=True,
    ).astype(jnp.bfloat16)
    return (prefill_out, decode_out)


def fast_layout(devices, prefill_rows, decode_rows, query_weight):
    planes = devices // 4
    tokens = prefill_rows.shape[0] + decode_rows.shape[1]
    return (
        planes * 4 == devices
        and planes & (planes - 1) == 0
        and prefill_rows.shape[0] == 1
        and decode_rows.shape[0] == 1
        and tokens == 4
        and query_weight.shape[1] == 3 * HEAD_DIM
    )


def dispatch(prefill_rows, decode_rows, kv_cache, lengths, slot, gain, query, keyval, output):
    devices = lax.axis_size("narrow")
    fast = fast_layout(devices, prefill_rows, decode_rows, query)
    body = per_device if fast else per_device_general
    return body(prefill_rows, decode_rows, kv_cache, lengths, slot, gain, query, keyval, output)


def solution(mesh):
    in_specs = (
        P(("group", "narrow"), None),
        P(("group", "narrow"), None, None),
        P(("group", "narrow"), None, None),
        P(("group", "narrow")),
        P("group"),
        P(),
        P(None, "narrow"),
        P("narrow", None),
        P("narrow", None),
    )
    out_specs = (P(("group", "narrow"), None), P(("group", "narrow"), None, None))
    return jax.shard_map(
        dispatch, mesh=mesh, in_specs=in_specs, out_specs=out_specs, check_vma=False
    )
```

```python
import functools

import jax
import jax.numpy as jnp
from jax import lax
from jax.experimental import pallas as pl
from jax.experimental.pallas import tpu as pltpu
from jax.sharding import PartitionSpec as P

HEAD_DIM = 128
EPSILON = 1e-05
CHUNK_ROWS = 32
BACK_ROWS = 16
VMEM_LIMIT = 24 << 20
LARGE_LIMIT = 52 << 20


def params():
    return pltpu.CompilerParams(vmem_limit_bytes=VMEM_LIMIT)


def cost(flops, bytes_accessed):
    return pl.CostEstimate(flops=flops, bytes_accessed=bytes_accessed, transcendentals=0)


def smem():
    return pl.BlockSpec(memory_space=pltpu.SMEM)


def vmem():
    return pl.BlockSpec(memory_space=pltpu.VMEM)


def norm_kernel(rank_ref, packed_ref, out_ref):
    tokens = out_ref.shape[0]
    rows = packed_ref[0, :tokens]
    center = rows - jnp.mean(rows, axis=-1, keepdims=True)
    spread = jnp.mean(center * center, axis=-1, keepdims=True)
    gain = packed_ref[0, tokens : tokens + 1]
    out_ref[...] = (center * lax.rsqrt(spread + EPSILON) * gain).astype(jnp.bfloat16)


def stack_kernel(slot_ref, length_ref, *refs):
    for i, ref in enumerate(refs[:-1]):
        refs[-1][i] = ref[...]


def add_kernel(keep_ref, other_ref, out_ref):
    out_ref[...] = (keep_ref[...] + other_ref[...].astype(jnp.float32)).astype(jnp.bfloat16)


def finish_kernel(keep_ref, side_ref, *refs):
    far_refs, (pre_hbm, dec_hbm, pre_ref, dec_ref, sem) = refs[:-5], refs[-5:]
    total = keep_ref[...] + side_ref[...].astype(jnp.float32)
    for far in far_refs:
        total = total + far[...].astype(jnp.float32)
    total = total.astype(jnp.bfloat16)
    pre_ref[...] = total[:1]
    dec_ref[0] = total[1:]
    copies = [
        pltpu.make_async_copy(pre_ref, pre_hbm, sem.at[0]),
        pltpu.make_async_copy(dec_ref, dec_hbm, sem.at[1]),
    ]
    for copy in copies:
        copy.start()
    for copy in copies:
        copy.wait()


def query_kernel(offsets, picks, rank_ref, *refs):
    block_refs, (weight_ref, kv_weight_ref, out_ref, own_ref) = refs[:-4], refs[-4:]
    rank = rank_ref[0]
    depth = kv_weight_ref.shape[0]
    owners = len(offsets)
    piece_refs = [block_refs[i] if k is None else block_refs[i].at[k] for i, k in picks]
    tokens = piece_refs[0].shape[0]
    heads = weight_ref.shape[1] // HEAD_DIM
    lhs = jnp.concatenate([p[...] for p in piece_refs], axis=0)
    queries = jnp.dot(lhs, weight_ref[...], preferred_element_type=jnp.float32)
    for h in range(heads):
        own_ref[h] = queries[:, h * HEAD_DIM : (h + 1) * HEAD_DIM].astype(jnp.bfloat16)
    start = pl.multiple_of(rank * depth, 128)
    part = jnp.concatenate([p[:, pl.ds(start, depth)] for p in piece_refs], axis=0)
    keyvals = jnp.dot(part, kv_weight_ref[...], preferred_element_type=jnp.float32)
    high = keyvals.astype(jnp.bfloat16).astype(jnp.float32)
    low = keyvals - high

    def piece(values, index):
        return values[:, index * HEAD_DIM : (index + 1) * HEAD_DIM].reshape(owners, tokens, HEAD_DIM)

    pieces = [piece(queries, h) for h in range(heads)]
    pieces += [piece(high, 0), piece(low, 0), piece(high, 1), piece(low, 1)]
    pad = CHUNK_ROWS - len(pieces) * tokens
    pieces.append(jnp.zeros((owners, pad, HEAD_DIM), jnp.float32))
    chunks = jnp.concatenate(pieces, axis=1).astype(jnp.bfloat16)
    for index, offset in enumerate(offsets):
        out_ref[rank ^ offset] = chunks[index]


def attend_kernel(rank_ref, slot_ref, length_ref, recv_ref, cache_ref, out_ref):
    owners = recv_ref.shape[0]
    tokens = 4
    heads = 3
    rows = 4 * (heads + 1)
    base = heads * tokens
    queries = recv_ref[:, :rows, :].reshape(owners * rows, HEAD_DIM)
    sums = jnp.sum(recv_ref[:, base : base + 4 * tokens, :].astype(jnp.float32), axis=0)
    key = (sums[0:tokens] + sums[tokens : 2 * tokens]).astype(jnp.bfloat16)
    value = (sums[2 * tokens : 3 * tokens] + sums[3 * tokens :]).astype(jnp.bfloat16)
    scale = HEAD_DIM ** (-0.5)
    dims = (((1,), (1,)), ((), ()))
    scores = (
        lax.dot_general(
            queries, cache_ref[0, :, :HEAD_DIM], dims, preferred_element_type=jnp.float32
        )
        * scale
    )
    column = lax.broadcasted_iota(jnp.int32, scores.shape, 1)
    scores = jnp.where(column < length_ref[0], scores, -1e30)
    fresh_pad = jnp.zeros((HEAD_DIM - tokens, HEAD_DIM), jnp.bfloat16)
    fresh_key = jnp.concatenate([key, fresh_pad], axis=0)
    fresh_value = jnp.concatenate([value, fresh_pad], axis=0)
    fresh = lax.dot_general(queries, fresh_key, dims, preferred_element_type=jnp.float32) * scale
    token = lax.broadcasted_iota(jnp.int32, fresh.shape, 0) % tokens
    which = lax.broadcasted_iota(jnp.int32, fresh.shape, 1)
    fresh = jnp.where((which >= 1) & (which <= token), fresh, -1e30)
    highest = jnp.maximum(
        jnp.max(scores, axis=-1, keepdims=True), jnp.max(fresh, axis=-1, keepdims=True)
    )
    weights = jnp.exp(scores - highest)
    fresh_weights = jnp.exp(fresh - highest)
    total = jnp.sum(weights, axis=-1, keepdims=True) + jnp.sum(
        fresh_weights, axis=-1, keepdims=True
    )
    mixed = jnp.dot(
        weights.astype(jnp.bfloat16), cache_ref[0, :, HEAD_DIM:], preferred_element_type=jnp.float32
    ) + jnp.dot(fresh_weights.astype(jnp.bfloat16), fresh_value, preferred_element_type=jnp.float32)
    mixed = (mixed / total).reshape(owners, rows, HEAD_DIM)
    key = key.astype(jnp.float32)
    value = value.astype(jnp.float32)
    first = jnp.concatenate([key, value], axis=0)[None]
    first = jnp.broadcast_to(first, (owners, 2 * tokens, HEAD_DIM))
    first = jnp.where(rank_ref[0] == slot_ref[0], first, mixed[:, : 2 * tokens])
    tail = jnp.concatenate([key[:1], value[:1], key[2:]], axis=0)[None]
    tail = jnp.broadcast_to(tail, (owners, rows - base, HEAD_DIM))
    out_ref[...] = jnp.concatenate([first, mixed[:, 2 * tokens : base], tail], axis=1).astype(
        jnp.bfloat16
    )


def project_kernel(early, rank_ref, slot_ref, recv_ref, own_ref, weight_hbm, *refs):
    out_refs, (weight_ref, sem) = refs[:-2], refs[-2:]
    parts = sem.shape[0]
    span = weight_ref.shape[1] // parts

    def fetch(i):
        window = pl.ds(i * span, span)
        return pltpu.make_async_copy(weight_hbm.at[:, window], weight_ref.at[:, window], sem.at[i])

    for i in range(early):
        fetch(i).start()
    rank = rank_ref[0]
    slot = slot_ref[0]
    owners = recv_ref.shape[0]
    planes = owners // 4
    tokens = 4
    heads = own_ref.shape[0]
    base = heads * tokens
    order = [4 * plane + stack for stack in (0, 2, 1, 3) for plane in range(planes)]
    remote = jnp.stack([recv_ref[rank ^ x] for x in order]).astype(jnp.float32)
    rows = owners * tokens
    fresh = recv_ref[slot].astype(jnp.float32)
    pad = jnp.zeros((tokens, HEAD_DIM), jnp.float32)
    marks = recv_ref[:, base : base + tokens, :].astype(jnp.float32)
    keys = jnp.concatenate([marks[:, 0], fresh[:tokens], pad], axis=0).astype(jnp.bfloat16)
    values = jnp.concatenate([marks[:, 1], fresh[tokens : 2 * tokens], pad], axis=0)
    values = values.astype(jnp.bfloat16)
    shape = (rows, keys.shape[0])
    row = lax.broadcasted_iota(jnp.int32, shape, 0)
    column = lax.broadcasted_iota(jnp.int32, shape, 1)
    position = row // tokens
    stack = position // planes
    stack = (stack % 2) * 2 + stack // 2
    owner = rank ^ (4 * (position % planes) + stack)
    token = row % tokens
    which = column - owners
    is_slot = (token >= 1) & (owner == slot)
    allowed = (column < owners) & ((column <= owner) | is_slot)
    allowed = allowed | (is_slot & (which >= 1) & (which <= token))
    use_local = ((token == 0) | is_slot)[:, :1]
    scale = HEAD_DIM ** (-0.5)
    pieces = []
    for h in range(heads):
        scores = (
            lax.dot_general(
                own_ref[h], keys, (((1,), (1,)), ((), ())), preferred_element_type=jnp.float32
            )
            * scale
        )
        scores = jnp.where(allowed, scores, -1e30)
        weights = jnp.exp(scores - jnp.max(scores, axis=-1, keepdims=True))
        total = jnp.sum(weights, axis=-1, keepdims=True)
        mixed = (
            jnp.dot(weights.astype(jnp.bfloat16), values, preferred_element_type=jnp.float32)
            / total
        )
        far = remote[:, h * tokens : (h + 1) * tokens].reshape(rows, HEAD_DIM)
        pieces.append(jnp.where(use_local, mixed, far).astype(jnp.bfloat16))
    lhs = jnp.concatenate(pieces, axis=1)
    part = rows // 4

    for i in range(parts):
        fetch(i).wait()
        if i + early < parts:
            fetch(i + early).start()
        window = slice(i * span, (i + 1) * span)
        out = jnp.dot(lhs, weight_ref[:, window], preferred_element_type=jnp.float32)
        for j, ref in enumerate(out_refs):
            ref[:, window] = out[j * part : (j + 1) * part].astype(ref.dtype)


def per_device(
    prefill_rows,
    decode_rows,
    kv_cache,
    slot_lengths,
    prefill_slot,
    norm_gain,
    query_weight,
    keyval_weight,
    output_weight,
):
    devices = lax.axis_size("narrow")
    rank = lax.axis_index("narrow")
    rank_arr = rank.astype(jnp.int32).reshape(1)
    width = prefill_rows.shape[-1]
    planes = devices // 4
    tokens = prefill_rows.shape[0] + decode_rows.shape[1]

    def swap(values, offset):
        return lax.ppermute(values, "narrow", [(i, i ^ offset) for i in range(devices)])

    def exchange(values):
        return lax.all_to_all(values, "narrow", split_axis=0, concat_axis=0, tiled=True)

    hbm = pl.BlockSpec(memory_space=pltpu.HBM)
    dma = pltpu.SemaphoreType.DMA
    row = lax.broadcasted_iota(jnp.int32, (1, tokens + 1, width), 1)
    edges = ((0, 0, 0), (1, 1, 0), (0, 0, 0))
    packed = lax.pad(decode_rows, jnp.zeros((), jnp.bfloat16), edges)
    packed = jnp.where(row == 0, prefill_rows[None], packed).astype(jnp.float32)
    packed = jnp.where(row == tokens, norm_gain.reshape(1, 1, width), packed)
    own = pl.pallas_call(
        norm_kernel,
        out_shape=jax.ShapeDtypeStruct((tokens, width), jnp.bfloat16),
        in_specs=[smem(), vmem()],
        out_specs=vmem(),
        compiler_params=params(),
        name="norm",
    )(rank_arr, packed)

    order = list(range(planes - 1, 0, -1))
    line = {k: swap(own, 4 * k) for k in order}
    line[0] = own
    side = {k: swap(line[k], 2) for k in [0] + order}

    def stack(values):
        return pl.pallas_call(
            stack_kernel,
            out_shape=jax.ShapeDtypeStruct((len(values), tokens, width), jnp.bfloat16),
            in_specs=[smem()] * 2 + [vmem()] * len(values),
            out_specs=vmem(),
            compiler_params=params(),
            cost_estimate=cost(10**10, 1),
        )(prefill_slot, slot_lengths, *values)

    line_core = swap(stack([line[k] for k in range(planes)]), 1)
    early = [0] + order[:-1]
    side_core = swap(stack([side[k] for k in early]), 1)
    last_core = swap(side[1], 1)
    blocks = [line[k] for k in range(planes)] + [side[k] for k in range(planes)]
    blocks += [line_core, side_core, last_core]
    picks = [(i, None) for i in range(2 * planes)]
    picks += [(2 * planes, k) for k in range(planes)]
    picks += [
        (2 * planes + 1, early.index(k)) if k in early else (2 * planes + 2, None)
        for k in range(planes)
    ]
    offsets = [4 * k + part for part in (0, 2, 1, 3) for k in range(planes)]
    heads = query_weight.shape[1] // HEAD_DIM
    chunks, own_queries = pl.pallas_call(
        functools.partial(query_kernel, offsets, picks),
        out_shape=(
            jax.ShapeDtypeStruct((devices, CHUNK_ROWS, HEAD_DIM), jnp.bfloat16),
            jax.ShapeDtypeStruct((heads, devices * tokens, HEAD_DIM), jnp.bfloat16),
        ),
        in_specs=[smem()] + [vmem()] * (len(blocks) + 2),
        out_specs=(vmem(), vmem()),
        compiler_params=params(),
        cost_estimate=cost(10**8, query_weight.size * 2 + keyval_weight.size * 2),
        name="query",
    )(rank_arr, *blocks, query_weight, keyval_weight)
    received = exchange(chunks)
    back = pl.pallas_call(
        attend_kernel,
        out_shape=jax.ShapeDtypeStruct((devices, BACK_ROWS, HEAD_DIM), jnp.bfloat16),
        in_specs=[smem()] * 3 + [vmem()] * 2,
        out_specs=vmem(),
        compiler_params=params(),
        name="attend",
    )(rank_arr, prefill_slot, slot_lengths, received, kv_cache)
    returned = exchange(back)
    quarter = devices * tokens // 4
    near, far_side, near_core, side_core = pl.pallas_call(
        functools.partial(project_kernel, 5),
        out_shape=(
            jax.ShapeDtypeStruct((quarter, width), jnp.float32),
            jax.ShapeDtypeStruct((quarter, width), jnp.float32),
            jax.ShapeDtypeStruct((quarter, width), jnp.bfloat16),
            jax.ShapeDtypeStruct((quarter, width), jnp.bfloat16),
        ),
        in_specs=[smem()] * 2 + [vmem()] * 2 + [hbm],
        out_specs=(vmem(),) * 4,
        scratch_shapes=[
            pltpu.VMEM(output_weight.shape, jnp.bfloat16),
            dma((8,)),
        ],
        compiler_params=pltpu.CompilerParams(vmem_limit_bytes=LARGE_LIMIT),
        cost_estimate=cost(10**8, output_weight.size * 2),
        name="project",
    )(rank_arr, prefill_slot, returned, own_queries, output_weight)
    side_core = swap(side_core, 1)
    near_core = swap(near_core, 1)

    def piece(values, k):
        return values[k * tokens : (k + 1) * tokens]

    far_side = far_side + side_core.astype(jnp.float32)
    sides = {k: swap(piece(far_side, k).astype(jnp.bfloat16), 2) for k in order + [0]}
    near = near + near_core.astype(jnp.float32)
    fars = []
    for k in order:
        total = pl.pallas_call(
            add_kernel,
            out_shape=jax.ShapeDtypeStruct((tokens, width), jnp.bfloat16),
            in_specs=[vmem()] * 2,
            out_specs=vmem(),
            compiler_params=params(),
        )(piece(near, k), sides[k])
        fars.append(swap(total, 4 * k))
    pre, dec = pl.pallas_call(
        finish_kernel,
        out_shape=(
            jax.ShapeDtypeStruct(prefill_rows.shape, jnp.bfloat16),
            jax.ShapeDtypeStruct(decode_rows.shape, jnp.bfloat16),
        ),
        in_specs=[vmem()] * (2 + len(fars)),
        out_specs=(hbm, hbm),
        scratch_shapes=[
            pltpu.VMEM(prefill_rows.shape, jnp.bfloat16),
            pltpu.VMEM(decode_rows.shape, jnp.bfloat16),
            dma((2,)),
        ],
        compiler_params=params(),
        name="finish",
    )(piece(near, 0), sides[0], *fars)
    return pre, dec


def layer_norm(inputs, gain):
    values = inputs.astype(jnp.float32)
    center = values - jnp.mean(values, axis=-1, keepdims=True)
    spread = jnp.mean(center * center, axis=-1, keepdims=True)
    return (center * lax.rsqrt(spread + EPSILON) * gain).astype(jnp.bfloat16)


def merge_block(state, queries, keyvals, allowed):
    highest, total, accum = state
    scores = jnp.einsum(
        "srhd,skd->srhk", queries, keyvals[..., :HEAD_DIM], preferred_element_type=jnp.float32
    )
    scores = scores * HEAD_DIM ** (-0.5)
    masked = jnp.where(allowed, scores, -1e30)
    new_high = jnp.maximum(highest, jnp.max(masked, axis=-1))
    weights = jnp.where(allowed, jnp.exp(scores - new_high[..., None]), 0.0)
    factor = jnp.exp(highest - new_high)
    total = total * factor + jnp.sum(weights, axis=-1)
    update = jnp.einsum(
        "srhk,skd->srhd",
        weights.astype(jnp.bfloat16),
        keyvals[..., HEAD_DIM:],
        preferred_element_type=jnp.float32,
    )
    accum = accum * factor[..., None] + update
    return (new_high, total, accum)


def per_device_general(
    prefill_rows,
    decode_rows,
    kv_cache,
    slot_lengths,
    prefill_slot,
    norm_gain,
    query_weight,
    keyval_weight,
    output_weight,
):
    CACHE = kv_cache.shape[1]
    PRE_DEV = prefill_rows.shape[0]
    STEPS = decode_rows.shape[1]
    HEADS = prefill_rows.shape[1] // HEAD_DIM
    devices = lax.axis_size("narrow")
    rank = lax.axis_index("narrow")
    prefill_total = PRE_DEV * devices
    row_width = keyval_weight.shape[0]
    row_start = rank * row_width
    width = HEADS * HEAD_DIM
    slot_count = kv_cache.shape[0]
    gathered = lax.all_gather(prefill_rows, "narrow", axis=0, tiled=True)
    normed = layer_norm(gathered, norm_gain)
    query_local = jnp.dot(normed, query_weight, preferred_element_type=jnp.float32).astype(
        jnp.bfloat16
    )
    normed_part = lax.dynamic_slice_in_dim(normed, row_start, row_width, 1)
    partial_kv = jnp.dot(normed_part, keyval_weight, preferred_element_type=jnp.float32)
    keyvals = lax.psum(partial_kv, "narrow").astype(jnp.bfloat16)
    own_queries = lax.all_to_all(query_local, "narrow", split_axis=0, concat_axis=1, tiled=True)
    own_queries = own_queries.reshape(1, PRE_DEV, HEADS, HEAD_DIM)
    own_pos = rank * PRE_DEV + jnp.arange(PRE_DEV, dtype=jnp.int32)
    key_pos = jnp.arange(prefill_total, dtype=jnp.int32)
    allowed = (key_pos[None, :] <= own_pos[:, None])[None, :, None, :]
    start_state = (
        jnp.full((1, PRE_DEV, HEADS), -1e30, jnp.float32),
        jnp.zeros((1, PRE_DEV, HEADS), jnp.float32),
        jnp.zeros((1, PRE_DEV, HEADS, HEAD_DIM), jnp.float32),
    )
    highest, total, accum = merge_block(start_state, own_queries, keyvals[None], allowed)
    pre_mixed = (accum / total[..., None]).astype(jnp.bfloat16).reshape(PRE_DEV, width)
    pre_back = lax.all_to_all(pre_mixed, "narrow", split_axis=1, concat_axis=0, tiled=True)
    rows = pre_back
    prefill_out = lax.psum_scatter(
        jnp.dot(rows, output_weight, preferred_element_type=jnp.float32),
        "narrow",
        scatter_dimension=0,
        tiled=True,
    ).astype(jnp.bfloat16)
    slot_ids = rank * slot_count + jnp.arange(slot_count, dtype=jnp.int32)
    chosen = slot_ids == prefill_slot[0]
    live_length = jnp.where(chosen, prefill_total, slot_lengths)
    block = min(512, CACHE)
    padded_prefill = jnp.concatenate(
        [keyvals, jnp.zeros((block - prefill_total, 2 * HEAD_DIM), jnp.bfloat16)], axis=0
    )
    block_count = CACHE // block
    gathered = lax.all_gather(decode_rows, "narrow", axis=0, tiled=True)
    normed = layer_norm(gathered, norm_gain)
    query_local = jnp.einsum(
        "ste,ec->stc", normed, query_weight, preferred_element_type=jnp.float32
    ).astype(jnp.bfloat16)
    normed_part = lax.dynamic_slice_in_dim(normed, row_start, row_width, 2)
    partial_kv = jnp.einsum(
        "ste,ec->stc", normed_part, keyval_weight, preferred_element_type=jnp.float32
    )
    fresh = lax.psum_scatter(partial_kv, "narrow", scatter_dimension=0, tiled=True).astype(
        jnp.bfloat16
    )
    own_queries = lax.all_to_all(query_local, "narrow", split_axis=0, concat_axis=2, tiled=True)
    own_queries = own_queries.reshape(slot_count, STEPS, HEADS, HEAD_DIM)
    queries = own_queries
    query_rows = queries.shape[1]
    state = (
        jnp.full((slot_count, query_rows, HEADS), -1e30, jnp.float32),
        jnp.zeros((slot_count, query_rows, HEADS), jnp.float32),
        jnp.zeros((slot_count, query_rows, HEADS, HEAD_DIM), jnp.float32),
    )

    def visit(block_index, carry):
        start = block_index * block
        rows = lax.dynamic_slice_in_dim(kv_cache, start, block, 1)
        position = start + jnp.arange(block, dtype=jnp.int32)
        replace = jnp.logical_and(chosen[:, None, None], (position < prefill_total)[None, :, None])
        rows = jnp.where(replace, padded_prefill[None], rows)
        valid = position[None, :] < live_length[:, None]
        return merge_block(carry, queries, rows, valid[:, None, None, :])

    state = lax.fori_loop(0, block_count, visit, state)
    fresh_valid = (
        jnp.arange(STEPS, dtype=jnp.int32)[None, :] <= jnp.arange(STEPS, dtype=jnp.int32)[:, None]
    )
    highest, total, accum = merge_block(state, queries, fresh, fresh_valid[None, :, None, :])
    mixed = (accum / total[..., None]).astype(jnp.bfloat16).reshape(slot_count, STEPS, width)
    back = lax.all_to_all(mixed, "narrow", split_axis=2, concat_axis=0, tiled=True)
    rows = back
    decode_out = lax.psum_scatter(
        jnp.einsum("stc,ce->ste", rows, output_weight, preferred_element_type=jnp.float32),
        "narrow",
        scatter_dimension=0,
        tiled=True,
    ).astype(jnp.bfloat16)
    return (prefill_out, decode_out)


def fast_layout(devices, prefill_rows, decode_rows, query_weight):
    planes = devices // 4
    tokens = prefill_rows.shape[0] + decode_rows.shape[1]
    return (
        planes * 4 == devices
        and planes & (planes - 1) == 0
        and prefill_rows.shape[0] == 1
        and decode_rows.shape[0] == 1
        and tokens == 4
        and query_weight.shape[1] == 3 * HEAD_DIM
    )


def dispatch(prefill_rows, decode_rows, kv_cache, lengths, slot, gain, query, keyval, output):
    devices = lax.axis_size("narrow")
    fast = fast_layout(devices, prefill_rows, decode_rows, query)
    body = per_device if fast else per_device_general
    return body(
        prefill_rows, decode_rows, kv_cache, lengths, slot, gain, query, keyval, output
    )


def solution(mesh):
    in_specs = (
        P(("group", "narrow"), None),
        P(("group", "narrow"), None, None),
        P(("group", "narrow"), None, None),
        P(("group", "narrow")),
        P("group"),
        P(),
        P(None, "narrow"),
        P("narrow", None),
        P("narrow", None),
    )
    out_specs = (P(("group", "narrow"), None), P(("group", "narrow"), None, None))
    return jax.shard_map(
        dispatch, mesh=mesh, in_specs=in_specs, out_specs=out_specs, check_vma=False
    )
```

```python
import functools

import jax
import jax.numpy as jnp
from jax import lax
from jax.experimental import pallas as pl
from jax.experimental.pallas import tpu as pltpu
from jax.sharding import PartitionSpec as P

HEAD_DIM = 128
EPSILON = 1e-05
GATHER = ("z3", "z2", "z1", "y0", "y3", "y21", "c0123", "b03", "b21")
SCATTER = ("s", "n", "y3", "y2", "y1", "y0", "z3", "z2", "z1")
VMEM_LIMIT = 24 << 20
LARGE_LIMIT = 50 << 20
FIRST_SHARE = 2
FETCHES = 6
EARLY = 6


def params():
    return pltpu.CompilerParams(vmem_limit_bytes=VMEM_LIMIT)


def cost(flops, bytes_accessed):
    return pl.CostEstimate(flops=flops, bytes_accessed=bytes_accessed, transcendentals=0)


def smem():
    return pl.BlockSpec(memory_space=pltpu.SMEM)


def vmem():
    return pl.BlockSpec(memory_space=pltpu.VMEM)


def norm_kernel(rank_ref, packed_ref, out_ref):
    tokens = out_ref.shape[0]
    rows = packed_ref[:tokens]
    center = rows - jnp.mean(rows, axis=-1, keepdims=True)
    spread = jnp.mean(center * center, axis=-1, keepdims=True)
    gain = packed_ref[tokens : tokens + 1]
    out_ref[...] = (center * lax.rsqrt(spread + EPSILON) * gain).astype(jnp.bfloat16)


def fetch_kernel(weight_hbm, after_ref, out_ref, sem):
    source = weight_hbm.at[:, pl.ds(0, out_ref.shape[1])]
    copy = pltpu.make_async_copy(source, out_ref, sem)
    copy.start()
    copy.wait()


def stack_kernel(*refs):
    for i, ref in enumerate(refs[:-1]):
        refs[-1][i] = ref[...]


def add_kernel(keep_ref, other_ref, out_ref):
    out_ref[...] = (keep_ref[...] + other_ref[...].astype(jnp.float32)).astype(jnp.bfloat16)


def finish_kernel(keep_ref, side_ref, *refs):
    far_refs, (pre_hbm, dec_hbm, pre_ref, dec_ref, sem) = refs[:-5], refs[-5:]
    total = keep_ref[...] + side_ref[...].astype(jnp.float32)
    for far in far_refs:
        total = total + far[...].astype(jnp.float32)
    total = total.astype(jnp.bfloat16)
    pre_ref[...] = total[:1]
    dec_ref[0] = total[1:]
    copies = [
        pltpu.make_async_copy(pre_ref, pre_hbm, sem.at[0]),
        pltpu.make_async_copy(dec_ref, dec_hbm, sem.at[1]),
    ]
    for copy in copies:
        copy.start()
    for copy in copies:
        copy.wait()


def query_kernel(offsets, picks, rank_ref, slot_ref, length_ref, *refs):
    block_refs, (weight_ref, kv_weight_ref, out_ref, own_ref) = refs[:-4], refs[-4:]
    rank = rank_ref[0]
    depth = kv_weight_ref.shape[0]
    owners = len(offsets)
    piece_refs = [block_refs[i] if k is None else block_refs[i].at[k] for i, k in picks]
    tokens = piece_refs[0].shape[0]
    heads = weight_ref.shape[1] // HEAD_DIM
    lhs = jnp.concatenate([p[...] for p in piece_refs], axis=0)
    queries = jnp.dot(lhs, weight_ref[...], preferred_element_type=jnp.float32)
    own = [queries[:, h * HEAD_DIM : (h + 1) * HEAD_DIM] for h in range(heads)]
    own_ref[...] = jnp.concatenate(own, axis=0).astype(jnp.bfloat16)
    start = pl.multiple_of(rank * depth, 128)
    part = jnp.concatenate([p[:, pl.ds(start, depth)] for p in piece_refs], axis=0)
    keyvals = jnp.dot(part, kv_weight_ref[...], preferred_element_type=jnp.float32)
    high = keyvals.astype(jnp.bfloat16).astype(jnp.float32)
    low = keyvals - high

    parts = [queries, high[:, :HEAD_DIM], low[:, :HEAD_DIM], high[:, HEAD_DIM:], low[:, HEAD_DIM:]]
    chunks = jnp.concatenate(parts, axis=1).reshape(owners, tokens, -1).astype(jnp.bfloat16)
    for index, offset in enumerate(offsets):
        out_ref[rank ^ offset] = chunks[index]


def lanes(values, index):
    return values[..., index * HEAD_DIM : (index + 1) * HEAD_DIM]


def attend_kernel(rank_ref, slot_ref, length_ref, recv_ref, cache_ref, out_ref):
    owners, tokens, columns = recv_ref.shape
    heads = columns // HEAD_DIM - 4
    received = recv_ref[...].astype(jnp.float32)
    queries = [lanes(received, h).reshape(owners * tokens, HEAD_DIM) for h in range(heads)]
    queries = jnp.concatenate(queries, axis=0).astype(jnp.bfloat16)
    sums = jnp.sum(received[:, :, heads * HEAD_DIM :], axis=0)
    key = (lanes(sums, 0) + lanes(sums, 1)).astype(jnp.bfloat16)
    value = (lanes(sums, 2) + lanes(sums, 3)).astype(jnp.bfloat16)
    scale = HEAD_DIM ** (-0.5)
    dims = (((1,), (1,)), ((), ()))
    scores = (
        lax.dot_general(
            queries, cache_ref[0, :, :HEAD_DIM], dims, preferred_element_type=jnp.float32
        )
        * scale
    )
    column = lax.broadcasted_iota(jnp.int32, scores.shape, 1)
    scores = jnp.where(column < length_ref[0], scores, -1e30)
    fresh_pad = jnp.zeros((HEAD_DIM - tokens, HEAD_DIM), jnp.bfloat16)
    fresh_key = jnp.concatenate([key, fresh_pad], axis=0)
    fresh_value = jnp.concatenate([value, fresh_pad], axis=0)
    fresh = lax.dot_general(queries, fresh_key, dims, preferred_element_type=jnp.float32) * scale
    token = lax.broadcasted_iota(jnp.int32, fresh.shape, 0) % tokens
    which = lax.broadcasted_iota(jnp.int32, fresh.shape, 1)
    fresh = jnp.where((which >= 1) & (which <= token), fresh, -1e30)
    highest = jnp.maximum(
        jnp.max(scores, axis=-1, keepdims=True), jnp.max(fresh, axis=-1, keepdims=True)
    )
    weights = jnp.exp(scores - highest)
    fresh_weights = jnp.exp(fresh - highest)
    total = jnp.sum(weights, axis=-1, keepdims=True) + jnp.sum(
        fresh_weights, axis=-1, keepdims=True
    )
    mixed = jnp.dot(
        weights.astype(jnp.bfloat16), cache_ref[0, :, HEAD_DIM:], preferred_element_type=jnp.float32
    ) + jnp.dot(fresh_weights.astype(jnp.bfloat16), fresh_value, preferred_element_type=jnp.float32)
    mixed = (mixed / total).reshape(heads, owners, tokens, HEAD_DIM)
    parts = [mixed[h] for h in range(heads)]
    key = key.astype(jnp.float32)
    value = value.astype(jnp.float32)
    restarted = rank_ref[0] == slot_ref[0]
    parts[0] = jnp.where(restarted, key[None], parts[0])
    parts[1] = jnp.where(restarted, value[None], parts[1])
    marks = jnp.concatenate([key[:1], value[:1], jnp.zeros((tokens - 2, HEAD_DIM), jnp.float32)])
    parts.append(jnp.broadcast_to(marks[None], parts[0].shape))
    out_ref[...] = jnp.concatenate(parts, axis=-1).astype(jnp.bfloat16)


def project_kernel(early, rank_ref, slot_ref, recv_ref, own_ref, first_ref, weight_hbm, *refs):
    out_refs, (weight_ref, sem) = refs[:-2], refs[-2:]
    parts = sem.shape[0]
    first_cols = first_ref.shape[1]
    span = weight_ref.shape[1] // parts

    def fetch(i):
        source = weight_hbm.at[:, pl.ds(first_cols + i * span, span)]
        return pltpu.make_async_copy(source, weight_ref.at[:, pl.ds(i * span, span)], sem.at[i])

    for i in range(early):
        fetch(i).start()
    rank = rank_ref[0]
    slot = slot_ref[0]
    owners, tokens, _ = recv_ref.shape
    planes = owners // 4
    heads = own_ref.shape[0] // (owners * tokens)
    order = [4 * plane + stack for stack in (0, 2, 1, 3) for plane in range(planes)]
    remote = jnp.stack([recv_ref[rank ^ x] for x in order]).astype(jnp.float32)
    rows = owners * tokens
    fresh = recv_ref[slot].astype(jnp.float32)
    pad = jnp.zeros((tokens, HEAD_DIM), jnp.float32)
    marks = lanes(remote, heads)
    keys = jnp.concatenate([marks[:, 0], lanes(fresh, 0), pad], axis=0).astype(jnp.bfloat16)
    values = jnp.concatenate([marks[:, 1], lanes(fresh, 1), pad], axis=0)
    values = values.astype(jnp.bfloat16)
    shape = (heads * rows, keys.shape[0])
    row = lax.broadcasted_iota(jnp.int32, shape, 0)
    column = lax.broadcasted_iota(jnp.int32, shape, 1)
    position = row // tokens % owners
    stack = position // planes
    stack = (stack % 2) * 2 + stack // 2
    owner = rank ^ (4 * (position % planes) + stack)
    token = row % tokens
    which = column - owners
    is_slot = (token >= 1) & (owner == slot)
    place = column // planes
    place = (place % 2) * 2 + place // 2
    source = rank ^ (4 * (column % planes) + place)
    allowed = (column < owners) & ((source <= owner) | is_slot)
    allowed = allowed | (is_slot & (which >= 1) & (which <= token))
    use_local = ((token == 0) | is_slot)[:, :1]
    dims = (((1,), (1,)), ((), ()))
    scores = lax.dot_general(own_ref[...], keys, dims, preferred_element_type=jnp.float32)
    scores = jnp.where(allowed, scores * HEAD_DIM ** (-0.5), -1e30)
    weights = jnp.exp(scores - jnp.max(scores, axis=-1, keepdims=True))
    total = jnp.sum(weights, axis=-1, keepdims=True)
    mixed = jnp.dot(weights.astype(jnp.bfloat16), values, preferred_element_type=jnp.float32)
    far = [lanes(remote, h).reshape(rows, HEAD_DIM) for h in range(heads)]
    mixed = jnp.where(use_local, mixed / total, jnp.concatenate(far, axis=0)).astype(jnp.bfloat16)
    pieces = [mixed[h * rows : (h + 1) * rows] for h in range(heads)]
    lhs = jnp.concatenate(pieces, axis=1)
    part = rows // 4

    def store(start, weights):
        out = jnp.dot(lhs, weights, preferred_element_type=jnp.float32)
        for j, ref in enumerate(out_refs):
            window = slice(start, start + out.shape[1])
            ref[:, window] = out[j * part : (j + 1) * part].astype(ref.dtype)

    store(0, first_ref[...])
    for i in range(parts):
        fetch(i).wait()
        if i + early < parts:
            fetch(i + early).start()
        store(first_cols + i * span, weight_ref[:, i * span : (i + 1) * span])


def per_device(
    prefill_rows,
    decode_rows,
    kv_cache,
    slot_lengths,
    prefill_slot,
    norm_gain,
    query_weight,
    keyval_weight,
    output_weight,
):
    devices = lax.axis_size("narrow")
    rank = lax.axis_index("narrow")
    rank_arr = rank.astype(jnp.int32).reshape(1)
    width = prefill_rows.shape[-1]
    planes = devices // 4
    tokens = prefill_rows.shape[0] + decode_rows.shape[1]

    def swap(values, offset):
        return lax.ppermute(values, "narrow", [(i, i ^ offset) for i in range(devices)])

    def exchange(values):
        return lax.all_to_all(values, "narrow", split_axis=0, concat_axis=0, tiled=True)

    hbm = pl.BlockSpec(memory_space=pltpu.HBM)
    dma = pltpu.SemaphoreType.DMA

    def place(values, before):
        after = tokens + 1 - before - values.shape[0]
        return lax.pad(values, jnp.zeros((), values.dtype), ((before, after, 0), (0, 0, 0)))

    packed = (place(prefill_rows, 0) + place(decode_rows[0], 1)).astype(jnp.float32)
    packed = packed + place(norm_gain.reshape(1, width), tokens)
    own = pl.pallas_call(
        norm_kernel,
        out_shape=jax.ShapeDtypeStruct((tokens, width), jnp.bfloat16),
        in_specs=[smem(), vmem()],
        out_specs=vmem(),
        compiler_params=params(),
        name="norm",
    )(rank_arr, packed)

    def stack(values):
        return pl.pallas_call(
            stack_kernel,
            out_shape=jax.ShapeDtypeStruct((len(values), tokens, width), jnp.bfloat16),
            in_specs=[vmem()] * len(values),
            out_specs=vmem(),
            compiler_params=params(),
            cost_estimate=cost(10**10, 1),
        )(*values)

    line = {0: own}
    blocks, where = [own], {(0, 0): (0, None)}
    sides = {}

    def add_block(values, part, ks):
        for i, k in enumerate(ks):
            where[part, k] = (len(blocks), i if len(ks) > 1 else None)
        blocks.append(values)

    def join(values):
        return values[0] if len(values) == 1 else stack(values)

    for step in GATHER:
        ks = [int(c) for c in step[1:]]
        if step[0] == "z":
            line[ks[0]] = swap(own, 4 * ks[0])
            add_block(line[ks[0]], 0, ks)
        elif step[0] == "y":
            value = swap(join([line[k] for k in ks]), 2)
            add_block(value, 2, ks)
            for i, k in enumerate(ks):
                sides[k] = value[i] if len(ks) > 1 else value
        elif step[0] == "c":
            add_block(swap(join([line[k] for k in ks]), 1), 1, ks)
        elif step[0] == "b":
            owner = {k: where[2, k] for k in ks}
            index = owner[ks[0]][0]
            if len(ks) > 1 and all(owner[k] == (index, i) for i, k in enumerate(ks)):
                value = blocks[index]
            else:
                value = join([sides[k] for k in ks])
            if step == GATHER[-1]:
                first_cols = width // FIRST_SHARE
                first = pl.pallas_call(
                    fetch_kernel,
                    out_shape=jax.ShapeDtypeStruct((output_weight.shape[0], first_cols), jnp.bfloat16),
                    in_specs=[hbm, vmem()],
                    out_specs=vmem(),
                    scratch_shapes=[dma(())],
                    compiler_params=pltpu.CompilerParams(vmem_limit_bytes=LARGE_LIMIT),
                    cost_estimate=cost(10**8, output_weight.size),
                    name="fetch",
                )(output_weight, line[1])
                value, first = lax.optimization_barrier((value, first))
            add_block(swap(value, 1), 3, ks)
    prefill_slot, slot_lengths, _ = lax.optimization_barrier(
        (prefill_slot, slot_lengths, sides[0])
    )
    picks = [where[part, k] for part in (0, 2, 1, 3) for k in range(planes)]
    offsets = [4 * k + part for part in (0, 2, 1, 3) for k in range(planes)]
    heads = query_weight.shape[1] // HEAD_DIM
    chunks, own_queries = pl.pallas_call(
        functools.partial(query_kernel, offsets, picks),
        out_shape=(
            jax.ShapeDtypeStruct((devices, tokens, (heads + 4) * HEAD_DIM), jnp.bfloat16),
            jax.ShapeDtypeStruct((heads * devices * tokens, HEAD_DIM), jnp.bfloat16),
        ),
        in_specs=[smem()] * 3 + [vmem()] * (len(blocks) + 2),
        out_specs=(vmem(), vmem()),
        compiler_params=params(),
        cost_estimate=cost(10**8, query_weight.size * 2 + keyval_weight.size * 2),
        name="query",
    )(rank_arr, prefill_slot, slot_lengths, *blocks, query_weight, keyval_weight)
    received = exchange(chunks)
    back = pl.pallas_call(
        attend_kernel,
        out_shape=jax.ShapeDtypeStruct((devices, tokens, (heads + 1) * HEAD_DIM), jnp.bfloat16),
        in_specs=[smem()] * 3 + [vmem()] * 2,
        out_specs=vmem(),
        compiler_params=params(),
        name="attend",
    )(rank_arr, prefill_slot, slot_lengths, received, kv_cache)
    returned = exchange(back)
    quarter = devices * tokens // 4
    near, far_side, near_core, side_core = pl.pallas_call(
        functools.partial(project_kernel, EARLY),
        out_shape=(
            jax.ShapeDtypeStruct((quarter, width), jnp.float32),
            jax.ShapeDtypeStruct((quarter, width), jnp.float32),
            jax.ShapeDtypeStruct((quarter, width), jnp.bfloat16),
            jax.ShapeDtypeStruct((quarter, width), jnp.bfloat16),
        ),
        in_specs=[smem()] * 2 + [vmem()] * 3 + [hbm],
        out_specs=(vmem(),) * 4,
        scratch_shapes=[
            pltpu.VMEM((output_weight.shape[0], width - first_cols), jnp.bfloat16),
            dma((FETCHES,)),
        ],
        compiler_params=pltpu.CompilerParams(vmem_limit_bytes=LARGE_LIMIT),
        cost_estimate=cost(10**8, output_weight.size * 2),
        name="project",
    )(rank_arr, prefill_slot, returned, own_queries, first, output_weight)
    side_core = swap(side_core, 1)
    near_core = swap(near_core, 1)

    def piece(values, k):
        return values[k * tokens : (k + 1) * tokens]

    far_side = (far_side + side_core.astype(jnp.float32)).astype(jnp.bfloat16)
    near = near + near_core.astype(jnp.float32)
    came, fars = {}, []
    for step in SCATTER:
        ks = [int(c) for c in step[1:]]
        if not ks:
            continue
        if step[0] == "y":
            value = jnp.concatenate([piece(far_side, k) for k in ks], axis=0)
            value = swap(value, 2)
            came.update({k: piece(value, i) for i, k in enumerate(ks)})
            continue
        k = ks[0]
        total = pl.pallas_call(
            add_kernel,
            out_shape=jax.ShapeDtypeStruct((tokens, width), jnp.bfloat16),
            in_specs=[vmem()] * 2,
            out_specs=vmem(),
            compiler_params=params(),
        )(piece(near, k), came[k])
        fars.append(swap(total, 4 * k))
    pre, dec = pl.pallas_call(
        finish_kernel,
        out_shape=(
            jax.ShapeDtypeStruct(prefill_rows.shape, jnp.bfloat16),
            jax.ShapeDtypeStruct(decode_rows.shape, jnp.bfloat16),
        ),
        in_specs=[vmem()] * (2 + len(fars)),
        out_specs=(hbm, hbm),
        scratch_shapes=[
            pltpu.VMEM(prefill_rows.shape, jnp.bfloat16),
            pltpu.VMEM(decode_rows.shape, jnp.bfloat16),
            dma((2,)),
        ],
        compiler_params=params(),
        name="finish",
    )(piece(near, 0), came[0], *fars)
    return pre, dec


def layer_norm(inputs, gain):
    values = inputs.astype(jnp.float32)
    center = values - jnp.mean(values, axis=-1, keepdims=True)
    spread = jnp.mean(center * center, axis=-1, keepdims=True)
    return (center * lax.rsqrt(spread + EPSILON) * gain).astype(jnp.bfloat16)


def merge_block(state, queries, keyvals, allowed):
    highest, total, accum = state
    scores = jnp.einsum(
        "srhd,skd->srhk", queries, keyvals[..., :HEAD_DIM], preferred_element_type=jnp.float32
    )
    scores = scores * HEAD_DIM ** (-0.5)
    masked = jnp.where(allowed, scores, -1e30)
    new_high = jnp.maximum(highest, jnp.max(masked, axis=-1))
    weights = jnp.where(allowed, jnp.exp(scores - new_high[..., None]), 0.0)
    factor = jnp.exp(highest - new_high)
    total = total * factor + jnp.sum(weights, axis=-1)
    update = jnp.einsum(
        "srhk,skd->srhd",
        weights.astype(jnp.bfloat16),
        keyvals[..., HEAD_DIM:],
        preferred_element_type=jnp.float32,
    )
    accum = accum * factor[..., None] + update
    return (new_high, total, accum)


def per_device_general(
    prefill_rows,
    decode_rows,
    kv_cache,
    slot_lengths,
    prefill_slot,
    norm_gain,
    query_weight,
    keyval_weight,
    output_weight,
):
    CACHE = kv_cache.shape[1]
    PRE_DEV = prefill_rows.shape[0]
    STEPS = decode_rows.shape[1]
    HEADS = prefill_rows.shape[1] // HEAD_DIM
    devices = lax.axis_size("narrow")
    rank = lax.axis_index("narrow")
    prefill_total = PRE_DEV * devices
    row_width = keyval_weight.shape[0]
    row_start = rank * row_width
    width = HEADS * HEAD_DIM
    slot_count = kv_cache.shape[0]
    gathered = lax.all_gather(prefill_rows, "narrow", axis=0, tiled=True)
    normed = layer_norm(gathered, norm_gain)
    query_local = jnp.dot(normed, query_weight, preferred_element_type=jnp.float32).astype(
        jnp.bfloat16
    )
    normed_part = lax.dynamic_slice_in_dim(normed, row_start, row_width, 1)
    partial_kv = jnp.dot(normed_part, keyval_weight, preferred_element_type=jnp.float32)
    keyvals = lax.psum(partial_kv, "narrow").astype(jnp.bfloat16)
    own_queries = lax.all_to_all(query_local, "narrow", split_axis=0, concat_axis=1, tiled=True)
    own_queries = own_queries.reshape(1, PRE_DEV, HEADS, HEAD_DIM)
    own_pos = rank * PRE_DEV + jnp.arange(PRE_DEV, dtype=jnp.int32)
    key_pos = jnp.arange(prefill_total, dtype=jnp.int32)
    allowed = (key_pos[None, :] <= own_pos[:, None])[None, :, None, :]
    start_state = (
        jnp.full((1, PRE_DEV, HEADS), -1e30, jnp.float32),
        jnp.zeros((1, PRE_DEV, HEADS), jnp.float32),
        jnp.zeros((1, PRE_DEV, HEADS, HEAD_DIM), jnp.float32),
    )
    highest, total, accum = merge_block(start_state, own_queries, keyvals[None], allowed)
    pre_mixed = (accum / total[..., None]).astype(jnp.bfloat16).reshape(PRE_DEV, width)
    pre_back = lax.all_to_all(pre_mixed, "narrow", split_axis=1, concat_axis=0, tiled=True)
    rows = pre_back
    prefill_out = lax.psum_scatter(
        jnp.dot(rows, output_weight, preferred_element_type=jnp.float32),
        "narrow",
        scatter_dimension=0,
        tiled=True,
    ).astype(jnp.bfloat16)
    slot_ids = rank * slot_count + jnp.arange(slot_count, dtype=jnp.int32)
    chosen = slot_ids == prefill_slot[0]
    live_length = jnp.where(chosen, prefill_total, slot_lengths)
    block = min(512, CACHE)
    padded_prefill = jnp.concatenate(
        [keyvals, jnp.zeros((block - prefill_total, 2 * HEAD_DIM), jnp.bfloat16)], axis=0
    )
    block_count = CACHE // block
    gathered = lax.all_gather(decode_rows, "narrow", axis=0, tiled=True)
    normed = layer_norm(gathered, norm_gain)
    query_local = jnp.einsum(
        "ste,ec->stc", normed, query_weight, preferred_element_type=jnp.float32
    ).astype(jnp.bfloat16)
    normed_part = lax.dynamic_slice_in_dim(normed, row_start, row_width, 2)
    partial_kv = jnp.einsum(
        "ste,ec->stc", normed_part, keyval_weight, preferred_element_type=jnp.float32
    )
    fresh = lax.psum_scatter(partial_kv, "narrow", scatter_dimension=0, tiled=True).astype(
        jnp.bfloat16
    )
    own_queries = lax.all_to_all(query_local, "narrow", split_axis=0, concat_axis=2, tiled=True)
    own_queries = own_queries.reshape(slot_count, STEPS, HEADS, HEAD_DIM)
    queries = own_queries
    query_rows = queries.shape[1]
    state = (
        jnp.full((slot_count, query_rows, HEADS), -1e30, jnp.float32),
        jnp.zeros((slot_count, query_rows, HEADS), jnp.float32),
        jnp.zeros((slot_count, query_rows, HEADS, HEAD_DIM), jnp.float32),
    )

    def visit(block_index, carry):
        start = block_index * block
        rows = lax.dynamic_slice_in_dim(kv_cache, start, block, 1)
        position = start + jnp.arange(block, dtype=jnp.int32)
        replace = jnp.logical_and(chosen[:, None, None], (position < prefill_total)[None, :, None])
        rows = jnp.where(replace, padded_prefill[None], rows)
        valid = position[None, :] < live_length[:, None]
        return merge_block(carry, queries, rows, valid[:, None, None, :])

    state = lax.fori_loop(0, block_count, visit, state)
    fresh_valid = (
        jnp.arange(STEPS, dtype=jnp.int32)[None, :] <= jnp.arange(STEPS, dtype=jnp.int32)[:, None]
    )
    highest, total, accum = merge_block(state, queries, fresh, fresh_valid[None, :, None, :])
    mixed = (accum / total[..., None]).astype(jnp.bfloat16).reshape(slot_count, STEPS, width)
    back = lax.all_to_all(mixed, "narrow", split_axis=2, concat_axis=0, tiled=True)
    rows = back
    decode_out = lax.psum_scatter(
        jnp.einsum("stc,ce->ste", rows, output_weight, preferred_element_type=jnp.float32),
        "narrow",
        scatter_dimension=0,
        tiled=True,
    ).astype(jnp.bfloat16)
    return (prefill_out, decode_out)


def fast_layout(devices, prefill_rows, decode_rows, query_weight):
    planes = devices // 4
    tokens = prefill_rows.shape[0] + decode_rows.shape[1]
    return (
        planes == 4
        and planes * 4 == devices
        and prefill_rows.shape[0] == 1
        and decode_rows.shape[0] == 1
        and tokens == 4
        and query_weight.shape[1] == 3 * HEAD_DIM
    )


def dispatch(prefill_rows, decode_rows, kv_cache, lengths, slot, gain, query, keyval, output):
    devices = lax.axis_size("narrow")
    fast = fast_layout(devices, prefill_rows, decode_rows, query)
    body = per_device if fast else per_device_general
    return body(
        prefill_rows, decode_rows, kv_cache, lengths, slot, gain, query, keyval, output
    )


def solution(mesh):
    in_specs = (
        P(("group", "narrow"), None),
        P(("group", "narrow"), None, None),
        P(("group", "narrow"), None, None),
        P(("group", "narrow")),
        P("group"),
        P(),
        P(None, "narrow"),
        P("narrow", None),
        P("narrow", None),
    )
    out_specs = (P(("group", "narrow"), None), P(("group", "narrow"), None, None))
    return jax.shard_map(
        dispatch, mesh=mesh, in_specs=in_specs, out_specs=out_specs, check_vma=False
    )
```

```python
import functools

import jax
import jax.numpy as jnp
from jax import lax
from jax.experimental import pallas as pl
from jax.experimental.pallas import tpu as pltpu
from jax.sharding import PartitionSpec as P

HEAD_DIM = 128
EPSILON = 1e-05
GATHER = ("z3", "z2", "z1", "y0", "y3", "y21", "c0123", "b03", "b21")
SCATTER = ("s", "n", "y3", "y2", "y1", "y0", "z3", "z2", "z1")
VMEM_LIMIT = 24 << 20
LARGE_LIMIT = 50 << 20
FIRST_SHARE = 7
FETCHES = 5
EARLY = 5


def params():
    return pltpu.CompilerParams(vmem_limit_bytes=VMEM_LIMIT)


def cost(flops, bytes_accessed):
    return pl.CostEstimate(flops=flops, bytes_accessed=bytes_accessed, transcendentals=0)


def smem():
    return pl.BlockSpec(memory_space=pltpu.SMEM)


def vmem():
    return pl.BlockSpec(memory_space=pltpu.VMEM)


def norm_kernel(packed_ref, out_ref):
    tokens = out_ref.shape[0]
    rows = packed_ref[:tokens]
    center = rows - jnp.mean(rows, axis=-1, keepdims=True)
    spread = jnp.mean(center * center, axis=-1, keepdims=True)
    gain = packed_ref[tokens : tokens + 1]
    out_ref[...] = (center * lax.rsqrt(spread + EPSILON) * gain).astype(jnp.bfloat16)


def fetch_kernel(weight_hbm, after_ref, out_ref, sem):
    source = weight_hbm.at[:, pl.ds(0, out_ref.shape[1])]
    copy = pltpu.make_async_copy(source, out_ref, sem)
    copy.start()
    copy.wait()


def stack_kernel(*refs):
    for i, ref in enumerate(refs[:-1]):
        refs[-1][i] = ref[...]


def plane(ref, index):
    return (ref[...] if index is None else ref[index]).astype(jnp.float32)


def add_kernel(index, keep_ref, other_ref, out_ref):
    out_ref[...] = (keep_ref[...] + plane(other_ref, index)).astype(jnp.bfloat16)


def finish_kernel(index, keep_ref, side_ref, *refs):
    far_refs, (pre_hbm, dec_hbm, pre_ref, dec_ref, sem) = refs[:-5], refs[-5:]
    total = keep_ref[...] + plane(side_ref, index)
    for far in far_refs:
        total = total + far[...].astype(jnp.float32)
    total = total.astype(jnp.bfloat16)
    pre_ref[...] = total[:1]
    dec_ref[0] = total[1:]
    copies = [
        pltpu.make_async_copy(pre_ref, pre_hbm, sem.at[0]),
        pltpu.make_async_copy(dec_ref, dec_hbm, sem.at[1]),
    ]
    for copy in copies:
        copy.start()
    for copy in copies:
        copy.wait()


def query_kernel(offsets, picks, slot_ref, length_ref, *refs):
    block_refs, (weight_ref, kv_weight_ref, out_ref, own_ref) = refs[:-4], refs[-4:]
    rank = lax.axis_index("narrow")
    depth = kv_weight_ref.shape[0]
    owners = len(offsets)
    piece_refs = [block_refs[i] if k is None else block_refs[i].at[k] for i, k in picks]
    tokens = piece_refs[0].shape[0]
    heads = weight_ref.shape[1] // HEAD_DIM
    lhs = jnp.concatenate([p[...] for p in piece_refs], axis=0)
    queries = jnp.dot(lhs, weight_ref[...], preferred_element_type=jnp.float32)
    own = [queries[:, h * HEAD_DIM : (h + 1) * HEAD_DIM] for h in range(heads)]
    own_ref[...] = jnp.concatenate(own, axis=0).astype(jnp.bfloat16)
    start = pl.multiple_of(rank * depth, 128)
    part = jnp.concatenate([p[:, pl.ds(start, depth)] for p in piece_refs], axis=0)
    keyvals = jnp.dot(part, kv_weight_ref[...], preferred_element_type=jnp.float32)
    high = keyvals.astype(jnp.bfloat16).astype(jnp.float32)
    low = keyvals - high

    parts = [queries, high[:, :HEAD_DIM], low[:, :HEAD_DIM], high[:, HEAD_DIM:], low[:, HEAD_DIM:]]
    chunks = jnp.concatenate(parts, axis=1).reshape(owners, tokens, -1).astype(jnp.bfloat16)
    for index, offset in enumerate(offsets):
        out_ref[rank ^ offset] = chunks[index]


def lanes(values, index):
    return values[..., index * HEAD_DIM : (index + 1) * HEAD_DIM]


def attend_kernel(slot_ref, length_ref, recv_ref, cache_ref, out_ref):
    owners, tokens, columns = recv_ref.shape
    heads = columns // HEAD_DIM - 4
    received = recv_ref[...].astype(jnp.float32)
    queries = [lanes(received, h).reshape(owners * tokens, HEAD_DIM) for h in range(heads)]
    queries = jnp.concatenate(queries, axis=0).astype(jnp.bfloat16)
    sums = jnp.sum(received[:, :, heads * HEAD_DIM :], axis=0)
    key = (lanes(sums, 0) + lanes(sums, 1)).astype(jnp.bfloat16)
    value = (lanes(sums, 2) + lanes(sums, 3)).astype(jnp.bfloat16)
    scale = HEAD_DIM ** (-0.5)
    dims = (((1,), (1,)), ((), ()))
    scores = (
        lax.dot_general(
            queries, cache_ref[0, :, :HEAD_DIM], dims, preferred_element_type=jnp.float32
        )
        * scale
    )
    column = lax.broadcasted_iota(jnp.int32, scores.shape, 1)
    scores = jnp.where(column < length_ref[0], scores, -1e30)
    fresh_pad = jnp.zeros((HEAD_DIM - tokens, HEAD_DIM), jnp.bfloat16)
    fresh_key = jnp.concatenate([key, fresh_pad], axis=0)
    fresh_value = jnp.concatenate([value, fresh_pad], axis=0)
    fresh = lax.dot_general(queries, fresh_key, dims, preferred_element_type=jnp.float32) * scale
    token = lax.broadcasted_iota(jnp.int32, fresh.shape, 0) % tokens
    which = lax.broadcasted_iota(jnp.int32, fresh.shape, 1)
    fresh = jnp.where((which >= 1) & (which <= token), fresh, -1e30)
    highest = jnp.maximum(
        jnp.max(scores, axis=-1, keepdims=True), jnp.max(fresh, axis=-1, keepdims=True)
    )
    weights = jnp.exp(scores - highest)
    fresh_weights = jnp.exp(fresh - highest)
    total = jnp.sum(weights, axis=-1, keepdims=True) + jnp.sum(
        fresh_weights, axis=-1, keepdims=True
    )
    mixed = jnp.dot(
        weights.astype(jnp.bfloat16), cache_ref[0, :, HEAD_DIM:], preferred_element_type=jnp.float32
    ) + jnp.dot(fresh_weights.astype(jnp.bfloat16), fresh_value, preferred_element_type=jnp.float32)
    mixed = (mixed / total).reshape(heads, owners, tokens, HEAD_DIM)
    parts = [mixed[h] for h in range(heads)]
    key = key.astype(jnp.float32)
    value = value.astype(jnp.float32)
    restarted = lax.axis_index("narrow") == slot_ref[0]
    parts[0] = jnp.where(restarted, key[None], parts[0])
    parts[1] = jnp.where(restarted, value[None], parts[1])
    marks = jnp.concatenate([key[:1], value[:1], jnp.zeros((tokens - 2, HEAD_DIM), jnp.float32)])
    parts.append(jnp.broadcast_to(marks[None], parts[0].shape))
    out_ref[...] = jnp.concatenate(parts, axis=-1).astype(jnp.bfloat16)


def project_kernel(early, slot_ref, recv_ref, own_ref, first_ref, weight_hbm, *refs):
    out_refs, (weight_ref, sem) = refs[:-2], refs[-2:]
    parts = sem.shape[0]
    first_cols = first_ref.shape[1]
    span = weight_ref.shape[1] // parts

    def fetch(i):
        source = weight_hbm.at[:, pl.ds(first_cols + i * span, span)]
        return pltpu.make_async_copy(source, weight_ref.at[:, pl.ds(i * span, span)], sem.at[i])

    for i in range(early):
        fetch(i).start()
    rank = lax.axis_index("narrow")
    slot = slot_ref[0]
    owners, tokens, _ = recv_ref.shape
    planes = owners // 4
    heads = own_ref.shape[0] // (owners * tokens)
    order = [4 * plane + stack for stack in (0, 2, 1, 3) for plane in range(planes)]
    remote = jnp.stack([recv_ref[rank ^ x] for x in order]).astype(jnp.float32)
    rows = owners * tokens
    fresh = recv_ref[slot].astype(jnp.float32)
    pad = jnp.zeros((tokens, HEAD_DIM), jnp.float32)
    marks = lanes(remote, heads)
    keys = jnp.concatenate([marks[:, 0], lanes(fresh, 0), pad], axis=0).astype(jnp.bfloat16)
    values = jnp.concatenate([marks[:, 1], lanes(fresh, 1), pad], axis=0)
    values = values.astype(jnp.bfloat16)
    shape = (heads * rows, keys.shape[0])
    row = lax.broadcasted_iota(jnp.int32, shape, 0)
    column = lax.broadcasted_iota(jnp.int32, shape, 1)
    position = row // tokens % owners
    stack = position // planes
    stack = (stack % 2) * 2 + stack // 2
    owner = rank ^ (4 * (position % planes) + stack)
    token = row % tokens
    which = column - owners
    is_slot = (token >= 1) & (owner == slot)
    place = column // planes
    place = (place % 2) * 2 + place // 2
    source = rank ^ (4 * (column % planes) + place)
    allowed = (column < owners) & ((source <= owner) | is_slot)
    allowed = allowed | (is_slot & (which >= 1) & (which <= token))
    use_local = ((token == 0) | is_slot)[:, :1]
    dims = (((1,), (1,)), ((), ()))
    scores = lax.dot_general(own_ref[...], keys, dims, preferred_element_type=jnp.float32)
    scores = jnp.where(allowed, scores * HEAD_DIM ** (-0.5), -1e30)
    weights = jnp.exp(scores - jnp.max(scores, axis=-1, keepdims=True))
    total = jnp.sum(weights, axis=-1, keepdims=True)
    mixed = jnp.dot(weights.astype(jnp.bfloat16), values, preferred_element_type=jnp.float32)
    far = [lanes(remote, h).reshape(rows, HEAD_DIM) for h in range(heads)]
    mixed = jnp.where(use_local, mixed / total, jnp.concatenate(far, axis=0)).astype(jnp.bfloat16)
    pieces = [mixed[h * rows : (h + 1) * rows] for h in range(heads)]
    lhs = jnp.concatenate(pieces, axis=1)
    part = rows // 4

    def store(start, weights):
        out = jnp.dot(lhs, weights, preferred_element_type=jnp.float32)
        for j, ref in enumerate(out_refs):
            window = slice(start, start + out.shape[1])
            ref[:, window] = out[j * part : (j + 1) * part].astype(ref.dtype)

    store(0, first_ref[...])
    for i in range(parts):
        fetch(i).wait()
        if i + early < parts:
            fetch(i + early).start()
        store(first_cols + i * span, weight_ref[:, i * span : (i + 1) * span])


def per_device(
    prefill_rows,
    decode_rows,
    kv_cache,
    slot_lengths,
    prefill_slot,
    norm_gain,
    query_weight,
    keyval_weight,
    output_weight,
):
    devices = lax.axis_size("narrow")
    width = prefill_rows.shape[-1]
    planes = devices // 4
    tokens = prefill_rows.shape[0] + decode_rows.shape[1]

    def swap(values, offset):
        return lax.ppermute(values, "narrow", [(i, i ^ offset) for i in range(devices)])

    def exchange(values):
        return lax.all_to_all(values, "narrow", split_axis=0, concat_axis=0, tiled=True)

    hbm = pl.BlockSpec(memory_space=pltpu.HBM)
    dma = pltpu.SemaphoreType.DMA

    def place(values, before):
        after = tokens + 1 - before - values.shape[0]
        return lax.pad(values, jnp.zeros((), values.dtype), ((before, after, 0), (0, 0, 0)))

    packed = (place(prefill_rows, 0) + place(decode_rows[0], 1)).astype(jnp.float32)
    packed = packed + place(norm_gain.reshape(1, width), tokens)
    own = pl.pallas_call(
        norm_kernel,
        out_shape=jax.ShapeDtypeStruct((tokens, width), jnp.bfloat16),
        in_specs=[vmem()],
        out_specs=vmem(),
        compiler_params=params(),
        name="norm",
    )(packed)

    def stack(values):
        return pl.pallas_call(
            stack_kernel,
            out_shape=jax.ShapeDtypeStruct((len(values), tokens, width), jnp.bfloat16),
            in_specs=[vmem()] * len(values),
            out_specs=vmem(),
            compiler_params=params(),
            cost_estimate=cost(10**10, 1),
        )(*values)

    line = {0: own}
    blocks, where = [own], {(0, 0): (0, None)}
    sides = {}

    def add_block(values, part, ks):
        for i, k in enumerate(ks):
            where[part, k] = (len(blocks), i if len(ks) > 1 else None)
        blocks.append(values)

    def join(values):
        return values[0] if len(values) == 1 else stack(values)

    for step in GATHER:
        ks = [int(c) for c in step[1:]]
        if step[0] == "z":
            line[ks[0]] = swap(own, 4 * ks[0])
            add_block(line[ks[0]], 0, ks)
        elif step[0] == "y":
            value = swap(join([line[k] for k in ks]), 2)
            add_block(value, 2, ks)
            for i, k in enumerate(ks):
                sides[k] = value[i] if len(ks) > 1 else value
        elif step[0] == "c":
            add_block(swap(join([line[k] for k in ks]), 1), 1, ks)
        elif step[0] == "b":
            owner = {k: where[2, k] for k in ks}
            index = owner[ks[0]][0]
            if len(ks) > 1 and all(owner[k] == (index, i) for i, k in enumerate(ks)):
                value = blocks[index]
            else:
                value = join([sides[k] for k in ks])
            if step == GATHER[-1]:
                first_cols = width * FIRST_SHARE // 12
                first = pl.pallas_call(
                    fetch_kernel,
                    out_shape=jax.ShapeDtypeStruct((output_weight.shape[0], first_cols), jnp.bfloat16),
                    in_specs=[hbm, vmem()],
                    out_specs=vmem(),
                    scratch_shapes=[dma(())],
                    compiler_params=pltpu.CompilerParams(vmem_limit_bytes=LARGE_LIMIT),
                    cost_estimate=cost(10**8, output_weight.size),
                    name="fetch",
                )(output_weight, line[1])
                value, first = lax.optimization_barrier((value, first))
            add_block(swap(value, 1), 3, ks)
    prefill_slot, slot_lengths, _ = lax.optimization_barrier(
        (prefill_slot, slot_lengths, sides[0])
    )
    picks = [where[part, k] for part in (0, 2, 1, 3) for k in range(planes)]
    offsets = [4 * k + part for part in (0, 2, 1, 3) for k in range(planes)]
    heads = query_weight.shape[1] // HEAD_DIM
    chunks, own_queries = pl.pallas_call(
        functools.partial(query_kernel, offsets, picks),
        out_shape=(
            jax.ShapeDtypeStruct((devices, tokens, (heads + 4) * HEAD_DIM), jnp.bfloat16),
            jax.ShapeDtypeStruct((heads * devices * tokens, HEAD_DIM), jnp.bfloat16),
        ),
        in_specs=[smem()] * 2 + [vmem()] * (len(blocks) + 2),
        out_specs=(vmem(), vmem()),
        compiler_params=params(),
        cost_estimate=cost(10**8, query_weight.size * 2 + keyval_weight.size * 2),
        name="query",
    )(prefill_slot, slot_lengths, *blocks, query_weight, keyval_weight)
    received = exchange(chunks)
    back = pl.pallas_call(
        attend_kernel,
        out_shape=jax.ShapeDtypeStruct((devices, tokens, (heads + 1) * HEAD_DIM), jnp.bfloat16),
        in_specs=[smem()] * 2 + [vmem()] * 2,
        out_specs=vmem(),
        compiler_params=params(),
        name="attend",
    )(prefill_slot, slot_lengths, received, kv_cache)
    returned = exchange(back)
    quarter = devices * tokens // 4
    near, far_side, near_core, side_core = pl.pallas_call(
        functools.partial(project_kernel, EARLY),
        out_shape=(
            jax.ShapeDtypeStruct((quarter, width), jnp.float32),
            jax.ShapeDtypeStruct((quarter, width), jnp.float32),
            jax.ShapeDtypeStruct((quarter, width), jnp.bfloat16),
            jax.ShapeDtypeStruct((quarter, width), jnp.bfloat16),
        ),
        in_specs=[smem()] + [vmem()] * 3 + [hbm],
        out_specs=(vmem(),) * 4,
        scratch_shapes=[
            pltpu.VMEM((output_weight.shape[0], width - first_cols), jnp.bfloat16),
            dma((FETCHES,)),
        ],
        compiler_params=pltpu.CompilerParams(vmem_limit_bytes=LARGE_LIMIT),
        cost_estimate=cost(10**8, output_weight.size * 2),
        name="project",
    )(prefill_slot, returned, own_queries, first, output_weight)
    side_core = swap(side_core, 1)
    near_core = swap(near_core, 1)

    def piece(values, k):
        return values[k * tokens : (k + 1) * tokens]

    far_side = (far_side + side_core.astype(jnp.float32)).astype(jnp.bfloat16)
    near = near + near_core.astype(jnp.float32)
    came, fars = {}, []
    for step in SCATTER:
        ks = [int(c) for c in step[1:]]
        if not ks:
            continue
        if step[0] == "y":
            value = join([piece(far_side, k) for k in ks])
            value = swap(value, 2)
            came.update({k: (i if len(ks) > 1 else None, value) for i, k in enumerate(ks)})
            continue
        k = ks[0]
        index, value = came[k]
        total = pl.pallas_call(
            functools.partial(add_kernel, index),
            out_shape=jax.ShapeDtypeStruct((tokens, width), jnp.bfloat16),
            in_specs=[vmem()] * 2,
            out_specs=vmem(),
            compiler_params=params(),
        )(piece(near, k), value)
        fars.append(swap(total, 4 * k))
    pre, dec = pl.pallas_call(
        functools.partial(finish_kernel, came[0][0]),
        out_shape=(
            jax.ShapeDtypeStruct(prefill_rows.shape, jnp.bfloat16),
            jax.ShapeDtypeStruct(decode_rows.shape, jnp.bfloat16),
        ),
        in_specs=[vmem()] * (2 + len(fars)),
        out_specs=(hbm, hbm),
        scratch_shapes=[
            pltpu.VMEM(prefill_rows.shape, jnp.bfloat16),
            pltpu.VMEM(decode_rows.shape, jnp.bfloat16),
            dma((2,)),
        ],
        compiler_params=params(),
        name="finish",
    )(piece(near, 0), came[0][1], *fars)
    return pre, dec


def layer_norm(inputs, gain):
    values = inputs.astype(jnp.float32)
    center = values - jnp.mean(values, axis=-1, keepdims=True)
    spread = jnp.mean(center * center, axis=-1, keepdims=True)
    return (center * lax.rsqrt(spread + EPSILON) * gain).astype(jnp.bfloat16)


def merge_block(state, queries, keyvals, allowed):
    highest, total, accum = state
    scores = jnp.einsum(
        "srhd,skd->srhk", queries, keyvals[..., :HEAD_DIM], preferred_element_type=jnp.float32
    )
    scores = scores * HEAD_DIM ** (-0.5)
    masked = jnp.where(allowed, scores, -1e30)
    new_high = jnp.maximum(highest, jnp.max(masked, axis=-1))
    weights = jnp.where(allowed, jnp.exp(scores - new_high[..., None]), 0.0)
    factor = jnp.exp(highest - new_high)
    total = total * factor + jnp.sum(weights, axis=-1)
    update = jnp.einsum(
        "srhk,skd->srhd",
        weights.astype(jnp.bfloat16),
        keyvals[..., HEAD_DIM:],
        preferred_element_type=jnp.float32,
    )
    accum = accum * factor[..., None] + update
    return (new_high, total, accum)


def per_device_general(
    prefill_rows,
    decode_rows,
    kv_cache,
    slot_lengths,
    prefill_slot,
    norm_gain,
    query_weight,
    keyval_weight,
    output_weight,
):
    CACHE = kv_cache.shape[1]
    PRE_DEV = prefill_rows.shape[0]
    STEPS = decode_rows.shape[1]
    HEADS = prefill_rows.shape[1] // HEAD_DIM
    devices = lax.axis_size("narrow")
    rank = lax.axis_index("narrow")
    prefill_total = PRE_DEV * devices
    row_width = keyval_weight.shape[0]
    row_start = rank * row_width
    width = HEADS * HEAD_DIM
    slot_count = kv_cache.shape[0]
    gathered = lax.all_gather(prefill_rows, "narrow", axis=0, tiled=True)
    normed = layer_norm(gathered, norm_gain)
    query_local = jnp.dot(normed, query_weight, preferred_element_type=jnp.float32).astype(
        jnp.bfloat16
    )
    normed_part = lax.dynamic_slice_in_dim(normed, row_start, row_width, 1)
    partial_kv = jnp.dot(normed_part, keyval_weight, preferred_element_type=jnp.float32)
    keyvals = lax.psum(partial_kv, "narrow").astype(jnp.bfloat16)
    own_queries = lax.all_to_all(query_local, "narrow", split_axis=0, concat_axis=1, tiled=True)
    own_queries = own_queries.reshape(1, PRE_DEV, HEADS, HEAD_DIM)
    own_pos = rank * PRE_DEV + jnp.arange(PRE_DEV, dtype=jnp.int32)
    key_pos = jnp.arange(prefill_total, dtype=jnp.int32)
    allowed = (key_pos[None, :] <= own_pos[:, None])[None, :, None, :]
    start_state = (
        jnp.full((1, PRE_DEV, HEADS), -1e30, jnp.float32),
        jnp.zeros((1, PRE_DEV, HEADS), jnp.float32),
        jnp.zeros((1, PRE_DEV, HEADS, HEAD_DIM), jnp.float32),
    )
    highest, total, accum = merge_block(start_state, own_queries, keyvals[None], allowed)
    pre_mixed = (accum / total[..., None]).astype(jnp.bfloat16).reshape(PRE_DEV, width)
    pre_back = lax.all_to_all(pre_mixed, "narrow", split_axis=1, concat_axis=0, tiled=True)
    rows = pre_back
    prefill_out = lax.psum_scatter(
        jnp.dot(rows, output_weight, preferred_element_type=jnp.float32),
        "narrow",
        scatter_dimension=0,
        tiled=True,
    ).astype(jnp.bfloat16)
    slot_ids = rank * slot_count + jnp.arange(slot_count, dtype=jnp.int32)
    chosen = slot_ids == prefill_slot[0]
    live_length = jnp.where(chosen, prefill_total, slot_lengths)
    block = min(512, CACHE)
    padded_prefill = jnp.concatenate(
        [keyvals, jnp.zeros((block - prefill_total, 2 * HEAD_DIM), jnp.bfloat16)], axis=0
    )
    block_count = CACHE // block
    gathered = lax.all_gather(decode_rows, "narrow", axis=0, tiled=True)
    normed = layer_norm(gathered, norm_gain)
    query_local = jnp.einsum(
        "ste,ec->stc", normed, query_weight, preferred_element_type=jnp.float32
    ).astype(jnp.bfloat16)
    normed_part = lax.dynamic_slice_in_dim(normed, row_start, row_width, 2)
    partial_kv = jnp.einsum(
        "ste,ec->stc", normed_part, keyval_weight, preferred_element_type=jnp.float32
    )
    fresh = lax.psum_scatter(partial_kv, "narrow", scatter_dimension=0, tiled=True).astype(
        jnp.bfloat16
    )
    own_queries = lax.all_to_all(query_local, "narrow", split_axis=0, concat_axis=2, tiled=True)
    own_queries = own_queries.reshape(slot_count, STEPS, HEADS, HEAD_DIM)
    queries = own_queries
    query_rows = queries.shape[1]
    state = (
        jnp.full((slot_count, query_rows, HEADS), -1e30, jnp.float32),
        jnp.zeros((slot_count, query_rows, HEADS), jnp.float32),
        jnp.zeros((slot_count, query_rows, HEADS, HEAD_DIM), jnp.float32),
    )

    def visit(block_index, carry):
        start = block_index * block
        rows = lax.dynamic_slice_in_dim(kv_cache, start, block, 1)
        position = start + jnp.arange(block, dtype=jnp.int32)
        replace = jnp.logical_and(chosen[:, None, None], (position < prefill_total)[None, :, None])
        rows = jnp.where(replace, padded_prefill[None], rows)
        valid = position[None, :] < live_length[:, None]
        return merge_block(carry, queries, rows, valid[:, None, None, :])

    state = lax.fori_loop(0, block_count, visit, state)
    fresh_valid = (
        jnp.arange(STEPS, dtype=jnp.int32)[None, :] <= jnp.arange(STEPS, dtype=jnp.int32)[:, None]
    )
    highest, total, accum = merge_block(state, queries, fresh, fresh_valid[None, :, None, :])
    mixed = (accum / total[..., None]).astype(jnp.bfloat16).reshape(slot_count, STEPS, width)
    back = lax.all_to_all(mixed, "narrow", split_axis=2, concat_axis=0, tiled=True)
    rows = back
    decode_out = lax.psum_scatter(
        jnp.einsum("stc,ce->ste", rows, output_weight, preferred_element_type=jnp.float32),
        "narrow",
        scatter_dimension=0,
        tiled=True,
    ).astype(jnp.bfloat16)
    return (prefill_out, decode_out)


def fast_layout(devices, prefill_rows, decode_rows, query_weight):
    planes = devices // 4
    tokens = prefill_rows.shape[0] + decode_rows.shape[1]
    return (
        planes == 4
        and planes * 4 == devices
        and prefill_rows.shape[0] == 1
        and decode_rows.shape[0] == 1
        and tokens == 4
        and query_weight.shape[1] == 3 * HEAD_DIM
    )


def dispatch(prefill_rows, decode_rows, kv_cache, lengths, slot, gain, query, keyval, output):
    devices = lax.axis_size("narrow")
    fast = fast_layout(devices, prefill_rows, decode_rows, query)
    body = per_device if fast else per_device_general
    return body(
        prefill_rows, decode_rows, kv_cache, lengths, slot, gain, query, keyval, output
    )


def solution(mesh):
    in_specs = (
        P(("group", "narrow"), None),
        P(("group", "narrow"), None, None),
        P(("group", "narrow"), None, None),
        P(("group", "narrow")),
        P("group"),
        P(),
        P(None, "narrow"),
        P("narrow", None),
        P("narrow", None),
    )
    out_specs = (P(("group", "narrow"), None), P(("group", "narrow"), None, None))
    return jax.shard_map(
        dispatch, mesh=mesh, in_specs=in_specs, out_specs=out_specs, check_vma=False
    )
```

```python
import functools

import jax
import jax.numpy as jnp
from jax import lax
from jax.experimental import pallas as pl
from jax.experimental.pallas import tpu as pltpu
from jax.sharding import PartitionSpec as P

HEAD_DIM = 128
EPSILON = 1e-05
GATHER = ("z3", "z2", "z1", "y0", "y3", "y21", "c0123", "b03", "b21")
SCATTER = ("s", "n", "y3", "y2", "y10", "z3", "z2", "z1")
VMEM_LIMIT = 24 << 20
LARGE_LIMIT = 50 << 20
FIRST_SHARE = 7
FETCHES = 5
EARLY = 5


def params():
    return pltpu.CompilerParams(vmem_limit_bytes=VMEM_LIMIT)


def cost(flops, bytes_accessed):
    return pl.CostEstimate(flops=flops, bytes_accessed=bytes_accessed, transcendentals=0)


def smem():
    return pl.BlockSpec(memory_space=pltpu.SMEM)


def vmem():
    return pl.BlockSpec(memory_space=pltpu.VMEM)


def norm_kernel(packed_ref, out_ref):
    tokens = out_ref.shape[0]
    rows = packed_ref[:tokens]
    center = rows - jnp.mean(rows, axis=-1, keepdims=True)
    spread = jnp.mean(center * center, axis=-1, keepdims=True)
    gain = packed_ref[tokens : tokens + 1]
    out_ref[...] = (center * lax.rsqrt(spread + EPSILON) * gain).astype(jnp.bfloat16)


def fetch_kernel(weight_hbm, after_ref, out_ref, sem):
    source = weight_hbm.at[:, pl.ds(0, out_ref.shape[1])]
    copy = pltpu.make_async_copy(source, out_ref, sem)
    copy.start()
    copy.wait()


def stack_kernel(*refs):
    for i, ref in enumerate(refs[:-1]):
        refs[-1][i] = ref[...]


def plane(ref, index):
    return (ref[...] if index is None else ref[index]).astype(jnp.float32)


def add_kernel(index, keep_ref, other_ref, out_ref):
    out_ref[...] = (keep_ref[...] + plane(other_ref, index)).astype(jnp.bfloat16)


def finish_kernel(index, keep_ref, side_ref, *refs):
    far_refs, (pre_hbm, dec_hbm, pre_ref, dec_ref, sem) = refs[:-5], refs[-5:]
    total = keep_ref[...] + plane(side_ref, index)
    for far in far_refs:
        total = total + far[...].astype(jnp.float32)
    total = total.astype(jnp.bfloat16)
    pre_ref[...] = total[:1]
    dec_ref[0] = total[1:]
    copies = [
        pltpu.make_async_copy(pre_ref, pre_hbm, sem.at[0]),
        pltpu.make_async_copy(dec_ref, dec_hbm, sem.at[1]),
    ]
    for copy in copies:
        copy.start()
    for copy in copies:
        copy.wait()


def query_kernel(offsets, picks, slot_ref, length_ref, *refs):
    block_refs, (weight_ref, kv_weight_ref, out_ref, own_ref) = refs[:-4], refs[-4:]
    rank = lax.axis_index("narrow")
    depth = kv_weight_ref.shape[0]
    owners = len(offsets)
    piece_refs = [block_refs[i] if k is None else block_refs[i].at[k] for i, k in picks]
    tokens = piece_refs[0].shape[0]
    heads = weight_ref.shape[1] // HEAD_DIM
    lhs = jnp.concatenate([p[...] for p in piece_refs], axis=0)
    queries = jnp.dot(lhs, weight_ref[...], preferred_element_type=jnp.float32)
    own = [queries[:, h * HEAD_DIM : (h + 1) * HEAD_DIM] for h in range(heads)]
    own_ref[...] = jnp.concatenate(own, axis=0).astype(jnp.bfloat16)
    start = pl.multiple_of(rank * depth, 128)
    part = jnp.concatenate([p[:, pl.ds(start, depth)] for p in piece_refs], axis=0)
    keyvals = jnp.dot(part, kv_weight_ref[...], preferred_element_type=jnp.float32)
    high = keyvals.astype(jnp.bfloat16).astype(jnp.float32)
    low = keyvals - high

    parts = [queries, high[:, :HEAD_DIM], low[:, :HEAD_DIM], high[:, HEAD_DIM:], low[:, HEAD_DIM:]]
    chunks = jnp.concatenate(parts, axis=1).reshape(owners, tokens, -1).astype(jnp.bfloat16)
    for index, offset in enumerate(offsets):
        out_ref[rank ^ offset] = chunks[index]


def lanes(values, index):
    return values[..., index * HEAD_DIM : (index + 1) * HEAD_DIM]


def attend_kernel(slot_ref, length_ref, recv_ref, cache_ref, out_ref):
    owners, tokens, columns = recv_ref.shape
    heads = columns // HEAD_DIM - 4
    received = recv_ref[...].astype(jnp.float32)
    queries = [lanes(received, h).reshape(owners * tokens, HEAD_DIM) for h in range(heads)]
    queries = jnp.concatenate(queries, axis=0).astype(jnp.bfloat16)
    sums = jnp.sum(received[:, :, heads * HEAD_DIM :], axis=0)
    key = (lanes(sums, 0) + lanes(sums, 1)).astype(jnp.bfloat16)
    value = (lanes(sums, 2) + lanes(sums, 3)).astype(jnp.bfloat16)
    scale = HEAD_DIM ** (-0.5)
    dims = (((1,), (1,)), ((), ()))
    scores = (
        lax.dot_general(
            queries, cache_ref[0, :, :HEAD_DIM], dims, preferred_element_type=jnp.float32
        )
        * scale
    )
    column = lax.broadcasted_iota(jnp.int32, scores.shape, 1)
    scores = jnp.where(column < length_ref[0], scores, -1e30)
    fresh_pad = jnp.zeros((HEAD_DIM - tokens, HEAD_DIM), jnp.bfloat16)
    fresh_key = jnp.concatenate([key, fresh_pad], axis=0)
    fresh_value = jnp.concatenate([value, fresh_pad], axis=0)
    fresh = lax.dot_general(queries, fresh_key, dims, preferred_element_type=jnp.float32) * scale
    token = lax.broadcasted_iota(jnp.int32, fresh.shape, 0) % tokens
    which = lax.broadcasted_iota(jnp.int32, fresh.shape, 1)
    fresh = jnp.where((which >= 1) & (which <= token), fresh, -1e30)
    highest = jnp.maximum(
        jnp.max(scores, axis=-1, keepdims=True), jnp.max(fresh, axis=-1, keepdims=True)
    )
    weights = jnp.exp(scores - highest)
    fresh_weights = jnp.exp(fresh - highest)
    total = jnp.sum(weights, axis=-1, keepdims=True) + jnp.sum(
        fresh_weights, axis=-1, keepdims=True
    )
    mixed = jnp.dot(
        weights.astype(jnp.bfloat16), cache_ref[0, :, HEAD_DIM:], preferred_element_type=jnp.float32
    ) + jnp.dot(fresh_weights.astype(jnp.bfloat16), fresh_value, preferred_element_type=jnp.float32)
    mixed = (mixed / total).reshape(heads, owners, tokens, HEAD_DIM)
    parts = [mixed[h] for h in range(heads)]
    key = key.astype(jnp.float32)
    value = value.astype(jnp.float32)
    restarted = lax.axis_index("narrow") == slot_ref[0]
    parts[0] = jnp.where(restarted, key[None], parts[0])
    parts[1] = jnp.where(restarted, value[None], parts[1])
    marks = jnp.concatenate([key[:1], value[:1], jnp.zeros((tokens - 2, HEAD_DIM), jnp.float32)])
    parts.append(jnp.broadcast_to(marks[None], parts[0].shape))
    out_ref[...] = jnp.concatenate(parts, axis=-1).astype(jnp.bfloat16)


def project_kernel(early, slot_ref, recv_ref, own_ref, first_ref, weight_hbm, *refs):
    out_refs, (weight_ref, sem) = refs[:-2], refs[-2:]
    parts = sem.shape[0]
    first_cols = first_ref.shape[1]
    span = weight_ref.shape[1] // parts

    def fetch(i):
        source = weight_hbm.at[:, pl.ds(first_cols + i * span, span)]
        return pltpu.make_async_copy(source, weight_ref.at[:, pl.ds(i * span, span)], sem.at[i])

    for i in range(early):
        fetch(i).start()
    rank = lax.axis_index("narrow")
    slot = slot_ref[0]
    owners, tokens, _ = recv_ref.shape
    planes = owners // 4
    heads = own_ref.shape[0] // (owners * tokens)
    order = [4 * plane + stack for stack in (0, 2, 1, 3) for plane in range(planes)]
    remote = jnp.stack([recv_ref[rank ^ x] for x in order]).astype(jnp.float32)
    rows = owners * tokens
    fresh = recv_ref[slot].astype(jnp.float32)
    pad = jnp.zeros((tokens, HEAD_DIM), jnp.float32)
    marks = lanes(remote, heads)
    keys = jnp.concatenate([marks[:, 0], lanes(fresh, 0), pad], axis=0).astype(jnp.bfloat16)
    values = jnp.concatenate([marks[:, 1], lanes(fresh, 1), pad], axis=0)
    values = values.astype(jnp.bfloat16)
    shape = (heads * rows, keys.shape[0])
    row = lax.broadcasted_iota(jnp.int32, shape, 0)
    column = lax.broadcasted_iota(jnp.int32, shape, 1)
    position = row // tokens % owners
    stack = position // planes
    stack = (stack % 2) * 2 + stack // 2
    owner = rank ^ (4 * (position % planes) + stack)
    token = row % tokens
    which = column - owners
    is_slot = (token >= 1) & (owner == slot)
    place = column // planes
    place = (place % 2) * 2 + place // 2
    source = rank ^ (4 * (column % planes) + place)
    allowed = (column < owners) & ((source <= owner) | is_slot)
    allowed = allowed | (is_slot & (which >= 1) & (which <= token))
    use_local = ((token == 0) | is_slot)[:, :1]
    dims = (((1,), (1,)), ((), ()))
    scores = lax.dot_general(own_ref[...], keys, dims, preferred_element_type=jnp.float32)
    scores = jnp.where(allowed, scores * HEAD_DIM ** (-0.5), -1e30)
    weights = jnp.exp(scores - jnp.max(scores, axis=-1, keepdims=True))
    total = jnp.sum(weights, axis=-1, keepdims=True)
    mixed = jnp.dot(weights.astype(jnp.bfloat16), values, preferred_element_type=jnp.float32)
    far = [lanes(remote, h).reshape(rows, HEAD_DIM) for h in range(heads)]
    mixed = jnp.where(use_local, mixed / total, jnp.concatenate(far, axis=0)).astype(jnp.bfloat16)
    pieces = [mixed[h * rows : (h + 1) * rows] for h in range(heads)]
    lhs = jnp.concatenate(pieces, axis=1)
    part = rows // 4

    def store(start, weights):
        out = jnp.dot(lhs, weights, preferred_element_type=jnp.float32)
        for j, ref in enumerate(out_refs):
            window = slice(start, start + out.shape[1])
            ref[:, window] = out[j * part : (j + 1) * part].astype(ref.dtype)

    for start in range(0, first_cols, span):
        store(start, first_ref[:, start : min(start + span, first_cols)])
    for i in range(parts):
        fetch(i).wait()
        if i + early < parts:
            fetch(i + early).start()
        store(first_cols + i * span, weight_ref[:, i * span : (i + 1) * span])


def per_device(
    prefill_rows,
    decode_rows,
    kv_cache,
    slot_lengths,
    prefill_slot,
    norm_gain,
    query_weight,
    keyval_weight,
    output_weight,
):
    devices = lax.axis_size("narrow")
    width = prefill_rows.shape[-1]
    planes = devices // 4
    tokens = prefill_rows.shape[0] + decode_rows.shape[1]

    def swap(values, offset):
        return lax.ppermute(values, "narrow", [(i, i ^ offset) for i in range(devices)])

    def exchange(values):
        return lax.all_to_all(values, "narrow", split_axis=0, concat_axis=0, tiled=True)

    hbm = pl.BlockSpec(memory_space=pltpu.HBM)
    dma = pltpu.SemaphoreType.DMA

    def place(values, before):
        after = tokens + 1 - before - values.shape[0]
        return lax.pad(values, jnp.zeros((), values.dtype), ((before, after, 0), (0, 0, 0)))

    packed = (place(prefill_rows, 0) + place(decode_rows[0], 1)).astype(jnp.float32)
    packed = packed + place(norm_gain.reshape(1, width), tokens)
    own = pl.pallas_call(
        norm_kernel,
        out_shape=jax.ShapeDtypeStruct((tokens, width), jnp.bfloat16),
        in_specs=[vmem()],
        out_specs=vmem(),
        compiler_params=params(),
        name="norm",
    )(packed)

    def stack(values):
        return pl.pallas_call(
            stack_kernel,
            out_shape=jax.ShapeDtypeStruct((len(values), tokens, width), jnp.bfloat16),
            in_specs=[vmem()] * len(values),
            out_specs=vmem(),
            compiler_params=params(),
            cost_estimate=cost(10**10, 1),
        )(*values)

    line = {0: own}
    blocks, where = [own], {(0, 0): (0, None)}
    sides = {}

    def add_block(values, part, ks):
        for i, k in enumerate(ks):
            where[part, k] = (len(blocks), i if len(ks) > 1 else None)
        blocks.append(values)

    def join(values):
        return values[0] if len(values) == 1 else stack(values)

    for step in GATHER:
        ks = [int(c) for c in step[1:]]
        if step[0] == "z":
            line[ks[0]] = swap(own, 4 * ks[0])
            add_block(line[ks[0]], 0, ks)
        elif step[0] == "y":
            value = swap(join([line[k] for k in ks]), 2)
            add_block(value, 2, ks)
            for i, k in enumerate(ks):
                sides[k] = value[i] if len(ks) > 1 else value
        elif step[0] == "c":
            add_block(swap(join([line[k] for k in ks]), 1), 1, ks)
        elif step[0] == "b":
            owner = {k: where[2, k] for k in ks}
            index = owner[ks[0]][0]
            if len(ks) > 1 and all(owner[k] == (index, i) for i, k in enumerate(ks)):
                value = blocks[index]
            else:
                value = join([sides[k] for k in ks])
            if step == GATHER[-1]:
                first_cols = width * FIRST_SHARE // 12
                first = pl.pallas_call(
                    fetch_kernel,
                    out_shape=jax.ShapeDtypeStruct((output_weight.shape[0], first_cols), jnp.bfloat16),
                    in_specs=[hbm, vmem()],
                    out_specs=vmem(),
                    scratch_shapes=[dma(())],
                    compiler_params=pltpu.CompilerParams(vmem_limit_bytes=LARGE_LIMIT),
                    cost_estimate=cost(10**8, output_weight.size),
                    name="fetch",
                )(output_weight, line[1])
                value, first = lax.optimization_barrier((value, first))
            add_block(swap(value, 1), 3, ks)
    prefill_slot, slot_lengths, _ = lax.optimization_barrier(
        (prefill_slot, slot_lengths, sides[0])
    )
    picks = [where[part, k] for part in (0, 2, 1, 3) for k in range(planes)]
    offsets = [4 * k + part for part in (0, 2, 1, 3) for k in range(planes)]
    heads = query_weight.shape[1] // HEAD_DIM
    chunks, own_queries = pl.pallas_call(
        functools.partial(query_kernel, offsets, picks),
        out_shape=(
            jax.ShapeDtypeStruct((devices, tokens, (heads + 4) * HEAD_DIM), jnp.bfloat16),
            jax.ShapeDtypeStruct((heads * devices * tokens, HEAD_DIM), jnp.bfloat16),
        ),
        in_specs=[smem()] * 2 + [vmem()] * (len(blocks) + 2),
        out_specs=(vmem(), vmem()),
        compiler_params=params(),
        cost_estimate=cost(10**8, query_weight.size * 2 + keyval_weight.size * 2),
        name="query",
    )(prefill_slot, slot_lengths, *blocks, query_weight, keyval_weight)
    received = exchange(chunks)
    back = pl.pallas_call(
        attend_kernel,
        out_shape=jax.ShapeDtypeStruct((devices, tokens, (heads + 1) * HEAD_DIM), jnp.bfloat16),
        in_specs=[smem()] * 2 + [vmem()] * 2,
        out_specs=vmem(),
        compiler_params=params(),
        name="attend",
    )(prefill_slot, slot_lengths, received, kv_cache)
    returned = exchange(back)
    quarter = devices * tokens // 4
    near, far_side, near_core, side_core = pl.pallas_call(
        functools.partial(project_kernel, EARLY),
        out_shape=(
            jax.ShapeDtypeStruct((quarter, width), jnp.float32),
            jax.ShapeDtypeStruct((quarter, width), jnp.float32),
            jax.ShapeDtypeStruct((quarter, width), jnp.bfloat16),
            jax.ShapeDtypeStruct((quarter, width), jnp.bfloat16),
        ),
        in_specs=[smem()] + [vmem()] * 3 + [hbm],
        out_specs=(vmem(),) * 4,
        scratch_shapes=[
            pltpu.VMEM((output_weight.shape[0], width - first_cols), jnp.bfloat16),
            dma((FETCHES,)),
        ],
        compiler_params=pltpu.CompilerParams(vmem_limit_bytes=LARGE_LIMIT),
        cost_estimate=cost(10**8, output_weight.size * 2),
        name="project",
    )(prefill_slot, returned, own_queries, first, output_weight)
    side_core = swap(side_core, 1)
    near_core = swap(near_core, 1)

    def piece(values, k):
        return values[k * tokens : (k + 1) * tokens]

    far_side = (far_side + side_core.astype(jnp.float32)).astype(jnp.bfloat16)
    near = near + near_core.astype(jnp.float32)
    came, fars = {}, []
    for step in SCATTER:
        ks = [int(c) for c in step[1:]]
        if not ks:
            continue
        if step[0] == "y":
            value = join([piece(far_side, k) for k in ks])
            value = swap(value, 2)
            came.update({k: (i if len(ks) > 1 else None, value) for i, k in enumerate(ks)})
            continue
        k = ks[0]
        index, value = came[k]
        total = pl.pallas_call(
            functools.partial(add_kernel, index),
            out_shape=jax.ShapeDtypeStruct((tokens, width), jnp.bfloat16),
            in_specs=[vmem()] * 2,
            out_specs=vmem(),
            compiler_params=params(),
        )(piece(near, k), value)
        fars.append(swap(total, 4 * k))
    pre, dec = pl.pallas_call(
        functools.partial(finish_kernel, came[0][0]),
        out_shape=(
            jax.ShapeDtypeStruct(prefill_rows.shape, jnp.bfloat16),
            jax.ShapeDtypeStruct(decode_rows.shape, jnp.bfloat16),
        ),
        in_specs=[vmem()] * (2 + len(fars)),
        out_specs=(hbm, hbm),
        scratch_shapes=[
            pltpu.VMEM(prefill_rows.shape, jnp.bfloat16),
            pltpu.VMEM(decode_rows.shape, jnp.bfloat16),
            dma((2,)),
        ],
        compiler_params=params(),
        name="finish",
    )(piece(near, 0), came[0][1], *fars)
    return pre, dec


def layer_norm(inputs, gain):
    values = inputs.astype(jnp.float32)
    center = values - jnp.mean(values, axis=-1, keepdims=True)
    spread = jnp.mean(center * center, axis=-1, keepdims=True)
    return (center * lax.rsqrt(spread + EPSILON) * gain).astype(jnp.bfloat16)


def merge_block(state, queries, keyvals, allowed):
    highest, total, accum = state
    scores = jnp.einsum(
        "srhd,skd->srhk", queries, keyvals[..., :HEAD_DIM], preferred_element_type=jnp.float32
    )
    scores = scores * HEAD_DIM ** (-0.5)
    masked = jnp.where(allowed, scores, -1e30)
    new_high = jnp.maximum(highest, jnp.max(masked, axis=-1))
    weights = jnp.where(allowed, jnp.exp(scores - new_high[..., None]), 0.0)
    factor = jnp.exp(highest - new_high)
    total = total * factor + jnp.sum(weights, axis=-1)
    update = jnp.einsum(
        "srhk,skd->srhd",
        weights.astype(jnp.bfloat16),
        keyvals[..., HEAD_DIM:],
        preferred_element_type=jnp.float32,
    )
    accum = accum * factor[..., None] + update
    return (new_high, total, accum)


def per_device_general(
    prefill_rows,
    decode_rows,
    kv_cache,
    slot_lengths,
    prefill_slot,
    norm_gain,
    query_weight,
    keyval_weight,
    output_weight,
):
    CACHE = kv_cache.shape[1]
    PRE_DEV = prefill_rows.shape[0]
    STEPS = decode_rows.shape[1]
    HEADS = prefill_rows.shape[1] // HEAD_DIM
    devices = lax.axis_size("narrow")
    rank = lax.axis_index("narrow")
    prefill_total = PRE_DEV * devices
    row_width = keyval_weight.shape[0]
    row_start = rank * row_width
    width = HEADS * HEAD_DIM
    slot_count = kv_cache.shape[0]
    gathered = lax.all_gather(prefill_rows, "narrow", axis=0, tiled=True)
    normed = layer_norm(gathered, norm_gain)
    query_local = jnp.dot(normed, query_weight, preferred_element_type=jnp.float32).astype(
        jnp.bfloat16
    )
    normed_part = lax.dynamic_slice_in_dim(normed, row_start, row_width, 1)
    partial_kv = jnp.dot(normed_part, keyval_weight, preferred_element_type=jnp.float32)
    keyvals = lax.psum(partial_kv, "narrow").astype(jnp.bfloat16)
    own_queries = lax.all_to_all(query_local, "narrow", split_axis=0, concat_axis=1, tiled=True)
    own_queries = own_queries.reshape(1, PRE_DEV, HEADS, HEAD_DIM)
    own_pos = rank * PRE_DEV + jnp.arange(PRE_DEV, dtype=jnp.int32)
    key_pos = jnp.arange(prefill_total, dtype=jnp.int32)
    allowed = (key_pos[None, :] <= own_pos[:, None])[None, :, None, :]
    start_state = (
        jnp.full((1, PRE_DEV, HEADS), -1e30, jnp.float32),
        jnp.zeros((1, PRE_DEV, HEADS), jnp.float32),
        jnp.zeros((1, PRE_DEV, HEADS, HEAD_DIM), jnp.float32),
    )
    highest, total, accum = merge_block(start_state, own_queries, keyvals[None], allowed)
    pre_mixed = (accum / total[..., None]).astype(jnp.bfloat16).reshape(PRE_DEV, width)
    pre_back = lax.all_to_all(pre_mixed, "narrow", split_axis=1, concat_axis=0, tiled=True)
    rows = pre_back
    prefill_out = lax.psum_scatter(
        jnp.dot(rows, output_weight, preferred_element_type=jnp.float32),
        "narrow",
        scatter_dimension=0,
        tiled=True,
    ).astype(jnp.bfloat16)
    slot_ids = rank * slot_count + jnp.arange(slot_count, dtype=jnp.int32)
    chosen = slot_ids == prefill_slot[0]
    live_length = jnp.where(chosen, prefill_total, slot_lengths)
    block = min(512, CACHE)
    padded_prefill = jnp.concatenate(
        [keyvals, jnp.zeros((block - prefill_total, 2 * HEAD_DIM), jnp.bfloat16)], axis=0
    )
    block_count = CACHE // block
    gathered = lax.all_gather(decode_rows, "narrow", axis=0, tiled=True)
    normed = layer_norm(gathered, norm_gain)
    query_local = jnp.einsum(
        "ste,ec->stc", normed, query_weight, preferred_element_type=jnp.float32
    ).astype(jnp.bfloat16)
    normed_part = lax.dynamic_slice_in_dim(normed, row_start, row_width, 2)
    partial_kv = jnp.einsum(
        "ste,ec->stc", normed_part, keyval_weight, preferred_element_type=jnp.float32
    )
    fresh = lax.psum_scatter(partial_kv, "narrow", scatter_dimension=0, tiled=True).astype(
        jnp.bfloat16
    )
    own_queries = lax.all_to_all(query_local, "narrow", split_axis=0, concat_axis=2, tiled=True)
    own_queries = own_queries.reshape(slot_count, STEPS, HEADS, HEAD_DIM)
    queries = own_queries
    query_rows = queries.shape[1]
    state = (
        jnp.full((slot_count, query_rows, HEADS), -1e30, jnp.float32),
        jnp.zeros((slot_count, query_rows, HEADS), jnp.float32),
        jnp.zeros((slot_count, query_rows, HEADS, HEAD_DIM), jnp.float32),
    )

    def visit(block_index, carry):
        start = block_index * block
        rows = lax.dynamic_slice_in_dim(kv_cache, start, block, 1)
        position = start + jnp.arange(block, dtype=jnp.int32)
        replace = jnp.logical_and(chosen[:, None, None], (position < prefill_total)[None, :, None])
        rows = jnp.where(replace, padded_prefill[None], rows)
        valid = position[None, :] < live_length[:, None]
        return merge_block(carry, queries, rows, valid[:, None, None, :])

    state = lax.fori_loop(0, block_count, visit, state)
    fresh_valid = (
        jnp.arange(STEPS, dtype=jnp.int32)[None, :] <= jnp.arange(STEPS, dtype=jnp.int32)[:, None]
    )
    highest, total, accum = merge_block(state, queries, fresh, fresh_valid[None, :, None, :])
    mixed = (accum / total[..., None]).astype(jnp.bfloat16).reshape(slot_count, STEPS, width)
    back = lax.all_to_all(mixed, "narrow", split_axis=2, concat_axis=0, tiled=True)
    rows = back
    decode_out = lax.psum_scatter(
        jnp.einsum("stc,ce->ste", rows, output_weight, preferred_element_type=jnp.float32),
        "narrow",
        scatter_dimension=0,
        tiled=True,
    ).astype(jnp.bfloat16)
    return (prefill_out, decode_out)


def fast_layout(devices, prefill_rows, decode_rows, query_weight):
    planes = devices // 4
    tokens = prefill_rows.shape[0] + decode_rows.shape[1]
    return (
        planes == 4
        and planes * 4 == devices
        and prefill_rows.shape[0] == 1
        and decode_rows.shape[0] == 1
        and tokens == 4
        and query_weight.shape[1] == 3 * HEAD_DIM
    )


def dispatch(prefill_rows, decode_rows, kv_cache, lengths, slot, gain, query, keyval, output):
    devices = lax.axis_size("narrow")
    fast = fast_layout(devices, prefill_rows, decode_rows, query)
    body = per_device if fast else per_device_general
    return body(
        prefill_rows, decode_rows, kv_cache, lengths, slot, gain, query, keyval, output
    )


def solution(mesh):
    in_specs = (
        P(("group", "narrow"), None),
        P(("group", "narrow"), None, None),
        P(("group", "narrow"), None, None),
        P(("group", "narrow")),
        P("group"),
        P(),
        P(None, "narrow"),
        P("narrow", None),
        P("narrow", None),
    )
    out_specs = (P(("group", "narrow"), None), P(("group", "narrow"), None, None))
    return jax.shard_map(
        dispatch, mesh=mesh, in_specs=in_specs, out_specs=out_specs, check_vma=False
    )
```
